256 devices in a mesh: segment: 16 (over y_lo, x, core), ctx: 16 (over y_hi, z).
Axes of the slice: x: 4, y: 4 (y_hi: 2, y_lo: 2; y = y_hi * 2 + y_lo), z: 8, core: 2. Of those that a mesh axis runs over, the one named last changes fastest.
Arguments:
- carried_down: bfloat16 [16, 2048, 1408], P('segment', 'ctx'), may hold values from -6 to 6
- carried_up: bfloat16 [16, 2048, 1408], P('segment', 'ctx'), may hold values from -6 to 6
- skip_bank: bfloat16 [16, 3, 2048, 1408], P('segment', None, 'ctx'), may hold values from -6 to 6
- queue: bfloat16 [8, 2048, 1408], P(None, 'ctx'), may hold values from -6 to 6
- next_entry: int32 [8], replicated, may hold values from 0 to 7, each once
- skip_slot: int32 [2, 16], P(None, 'segment'), may hold values from 0 to 2
- w_qkv: bfloat16 [16, 3, 1408, 1408], P('segment', None, 'ctx'), may hold values from -1.6523056 to 1.6523056
- w_out: bfloat16 [16, 1408, 1408], P('segment', 'ctx'), may hold values from -0.5 to 0.5
- w_skip: bfloat16 [16, 2816, 1408], P('segment', 'ctx'), may hold values from -0.109375 to 0.109375
- gains: float32 [16, 2, 1408], P('segment'), may hold values from 0.1 to 1.9
Outputs:
- desc_out: bfloat16 [2, 16, 2048, 1408], P(None, 'segment', 'ctx')
- asc_out: bfloat16 [2, 16, 2048, 1408], P(None, 'segment', 'ctx')
The draws below stay inside these ranges and needn't reach their ends.
All inputs are finite; a program needn't handle non-finite values.
Results may differ from the reference program's by a relative error of at most 0.015.
Values may be sent and summed in bfloat16 or wider, within the bound.
A program may use at most 128 MiB of HBM per device.

```python
import math
import jax
import jax.numpy as jnp
from jax import lax

HEADS = 16
HEAD = 88
D = 1408
TOKENS = 2048
SEGMENTS = 16
TICKS = 2
SLOTS = 3
POOL = 8


def draw_w_qkv(key, part):
    first = jax.random.fold_in(jax.random.fold_in(key, 17), 0)
    factor = 1.2 / math.sqrt(D)
    base = jnp.clip(jax.random.normal(first, (SEGMENTS, 3, D, D), jnp.float32), -4.0, 4.0) * factor
    return base.astype(jnp.bfloat16)


def set_ends(drawn, key, smallest, high):
    longest = drawn.shape.index(max(drawn.shape))
    spots = []
    for shift in (0, 1):
        where = [jax.random.randint(jax.random.fold_in(key, axis), (), 0, length) for axis, length in enumerate(drawn.shape)]
        where[longest] = (where[longest] + shift) % drawn.shape[longest]
        spots.append(tuple(where))
    return drawn.at[spots[0]].set(smallest).at[spots[1]].set(high)


def shard_levels(stream_key, shape, cuts, least, high):
    def one(position, shards_of):
        draws = jax.random.uniform(jax.random.fold_in(jax.random.fold_in(stream_key, 6), position), (shards_of,), jnp.float32, least / len(cuts), high / len(cuts))
        return jnp.repeat(jnp.exp(draws), shape[position] // shards_of).reshape((-1,) + (1,) * (len(shape) - position - 1))

    loudness = one(*cuts[0])
    for cut in cuts[1:]:
        loudness = loudness * one(*cut)
    return loudness


def centred(key, extent, width, reach, shards=(), held_as=jnp.bfloat16):
    loudness = shard_levels(key, extent, shards, -0.22, 0.18) if shards else 1.0
    drawn = jax.random.normal(key, extent, jnp.float32) * width * loudness
    return jnp.minimum(jnp.maximum(drawn, -reach), reach).astype(held_as)


def setup_inputs(seed: int = 0) -> dict:
    seeds = jax.random.split(jax.random.key(seed), 11)
    carried_down = centred(seeds[0], (SEGMENTS, TOKENS, D), 1.0, 6.0, ((0, 16), (1, 16)))
    carried_up = centred(seeds[1], (SEGMENTS, TOKENS, D), 1.0, 6.0, ((0, 16), (1, 16)))
    skip_bank = centred(seeds[2], (SEGMENTS, SLOTS, TOKENS, D), 1.0, 6.0, ((0, 16), (2, 16)))
    queue = centred(seeds[3], (POOL, TOKENS, D), 1.0, 6.0, ((1, 16),))
    next_entry = jax.random.permutation(seeds[4], POOL).astype(jnp.int32)
    skip_slot = set_ends(jax.random.randint(seeds[5], (TICKS, SEGMENTS), 0, SLOTS), jax.random.fold_in(seeds[5], 1), 0, SLOTS - 1).astype(jnp.int32)
    w_qkv = draw_w_qkv(jax.random.fold_in(seeds[10], 71), 0)
    w_out = centred(seeds[7], (SEGMENTS, D, D), (D // 9) ** -0.5, 0.5, ((0, 16), (1, 16)))
    w_skip = centred(seeds[8], (SEGMENTS, 2 * D, D), (2 * D) ** -0.5, 0.109375, ((0, 16), (1, 16)))
    gains = jnp.clip(1.0 + 0.18 * jax.random.normal(seeds[9], (SEGMENTS, 2, D), jnp.float32), 0.1, 1.9)
    return {"carried_down": carried_down, "carried_up": carried_up, "skip_bank": skip_bank, "queue": queue, "next_entry": next_entry, "skip_slot": skip_slot, "w_qkv": w_qkv, "w_out": w_out, "w_skip": w_skip, "gains": gains}


def layer_norm(values, gain):
    center = values - lax.optimization_barrier(jnp.mean(values, axis=-1, keepdims=True))
    spread = lax.optimization_barrier(jnp.mean(center * center, axis=-1, keepdims=True))
    return center * lax.rsqrt(spread + 1e-06) * gain

def attend_head(operands):
    queries, keys, values = operands
    scores = jnp.dot(queries, keys.T, preferred_element_type=jnp.float32) * HEAD ** (-0.5)
    peak = lax.optimization_barrier(jnp.max(scores, axis=1, keepdims=True))
    powers = jnp.exp(scores - peak)
    totals = lax.optimization_barrier(jnp.sum(powers, axis=1, keepdims=True))
    mixed = jnp.dot(powers.astype(jnp.bfloat16), values, preferred_element_type=jnp.float32) / totals
    return mixed.astype(jnp.bfloat16)

def descend(inputs, w_qkv, w_out, gain):
    normed = layer_norm(inputs.astype(jnp.float32), gain).astype(jnp.bfloat16)
    pieces = []
    for which in range(3):
        proj = jnp.dot(normed, w_qkv[which].T, preferred_element_type=jnp.float32).astype(jnp.bfloat16)
        pieces.append(proj.reshape(TOKENS, HEADS, HEAD).transpose(1, 0, 2))
    mixed = lax.map(attend_head, (pieces[0], pieces[1], pieces[2]))
    merged = mixed.transpose(1, 0, 2).reshape(TOKENS, D)
    result = inputs.astype(jnp.float32) + jnp.dot(merged, w_out, preferred_element_type=jnp.float32)
    return result.astype(jnp.bfloat16)

def ascend(rising, skip, w_skip, gain):
    joined = jnp.concatenate([rising, skip], axis=1)
    projected = jnp.dot(joined, w_skip, preferred_element_type=jnp.float32)
    return layer_norm(projected, gain).astype(jnp.bfloat16)

def one_tick(down_in, up_in, skip_bank, slots, w_qkv, w_out, w_skip, gains):

    def per_segment(operands):
        down, rising, bank, slot, weight_qkv, weight_out, weight_skip, gain = operands
        skip = lax.dynamic_index_in_dim(bank, slot.astype(jnp.int32), 0, keepdims=False)
        return (descend(down, weight_qkv, weight_out, gain[0]), ascend(rising, skip, weight_skip, gain[1]))
    return lax.map(per_segment, (down_in, up_in, skip_bank, slots, w_qkv, w_out, w_skip, gains))

def reference(carried_down, carried_up, skip_bank, queue, next_entry, skip_slot, w_qkv, w_out, w_skip, gains):
    first_down, first_up = one_tick(carried_down, carried_up, skip_bank, skip_slot[0], w_qkv, w_out, w_skip, gains)
    entering = lax.dynamic_index_in_dim(queue, next_entry[0].astype(jnp.int32), 0, keepdims=True)
    down_next = jnp.concatenate([entering, first_down[:-1]], axis=0)
    up_next = jnp.concatenate([first_up[1:], first_down[-1:]], axis=0)
    second_down, second_up = one_tick(down_next, up_next, skip_bank, skip_slot[1], w_qkv, w_out, w_skip, gains)
    return (jnp.stack([first_down, second_down]), jnp.stack([first_up, second_up]))
```

```python
import jax
import jax.numpy as jnp
from jax import lax
from jax.experimental import pallas as pl
from jax.experimental.pallas import tpu as pltpu
from jax.sharding import PartitionSpec as P

HEAD = 88
HP = 96
D = 1408
TOK = 128
RING = 8
SEGS = 16
ROWS = 176
SCALE = HEAD**-0.5
LOG2E = 1.4426950408889634
MESH = pl.DeviceIdType.MESH
BF = jnp.bfloat16
F32 = jnp.float32
GROUPS = ((0, 1), (1, 3), (3, 5), (5, 7), (7, 8))


def slot_of(delta):
    if delta == 0:
        return 0
    if abs(delta) == 4:
        return 7
    return 2 * delta - 1 if delta > 0 else -2 * delta


def nt(a, b):
    return lax.dot_general(a, b, (((1,), (1,)), ((), ())), preferred_element_type=F32)


def tn(a, b):
    return lax.dot_general(a, b, (((0,), (0,)), ((), ())), preferred_element_type=F32)


def layer_norm(x, gain):
    center = x - jnp.mean(x, axis=-1, keepdims=True)
    spread = jnp.mean(center * center, axis=-1, keepdims=True)
    return center * lax.rsqrt(spread + 1e-06) * gain


class Ring:
    def __init__(self, peers, send, recv, src, dst):
        self.peers, self.send, self.recv, self.src, self.dst = peers, send, recv, src, dst

    def copy(self, way, j):
        hops, half = j // 2, (way if j == 6 else j % 2)
        return pltpu.make_async_remote_copy(
            self.src(way, hops, half),
            self.dst(way, hops, half),
            self.send.at[way, j],
            self.recv.at[way, j],
            device_id={"ctx": self.peers[way]},
            device_id_type=MESH,
        )

    def start(self, way, j):
        self.copy(way, j).start()

    def arrive(self, way, j):
        hops, half = j // 2, (way if j == 6 else j % 2)
        here = self.src(way, hops + 1, half)
        pltpu.make_async_remote_copy(
            here,
            here,
            self.send.at[way, j],
            self.recv.at[way, j],
            device_id={"ctx": self.peers[way]},
            device_id_type=MESH,
        ).wait_recv()

    def begin(self, half):
        self.start(0, half)
        self.start(1, half)

    def step(self, j):
        for way in (0, 1):
            self.arrive(way, j)
            if j < 4:
                self.start(way, j + 2)
            elif j == 4 + way:
                self.start(way, 6)

    def drain(self):
        for way in (0, 1):
            for j in range(7):
                self.copy(way, j).wait_send()


def slot_ring(peers, send, recv, view):
    def src(way, hops, half):
        return view(slot_of(-hops if way == 0 else hops), half)

    def dst(way, hops, half):
        return view(slot_of(-hops - 1 if way == 0 else hops + 1), half)

    return Ring(peers, send, recv, src, dst)


def row_ring(peers, send, recv, z, buf):
    def src(way, hops, half):
        origin = lax.rem(z + (8 - hops if way == 0 else hops), 8)
        start = pl.multiple_of(origin * ROWS + half * 96, 16)
        return buf.at[pl.ds(start, 80 if half else 96), :]

    return Ring(peers, send, recv, src, src)


def kernel(
    x_in, up_in, bank_in, queue_in, entry, slots, qkv_in, out_in, skip_in, gains,
    desc_ref, asc_ref,
    xs, down, bank, queue, stage_qkv, act, wqv, wk, qt, kk, vt, qs, ks, vs, scores, ot, mt,
    wo, wsk, part_send, part_recv, x1, operand, give, asc_send, asc_recv, asc_out,
    load, store, act_send, act_recv, wo_send, wo_recv, wsk_send, wsk_recv,
    pair_send, pair_recv, w_send, w_recv, head_send, head_recv,
    part_ss, part_rs, down_ss, down_rs, give_ss, give_rs, rise_ss, rise_rs, mix_ss, mix_rs,
):
    s = lax.axis_index("segment")
    c = lax.axis_index("ctx")
    y, z = c // 8, c % 8
    partner = (1 - y) * 8 + z
    above, below = (s + 1) % SEGS, (s + SEGS - 1) % SEGS

    def ring_peer(delta):
        return y * 8 + (z + delta + 8) % 8

    peers = (ring_peer(1), ring_peer(-1))

    loads = [
        pltpu.make_async_copy(x_in, xs.at[0], load.at[0]),
        pltpu.make_async_copy(qkv_in, stage_qkv, load.at[1]),
        pltpu.make_async_copy(out_in, wo.at[0, pl.ds(0, HEAD), :], load.at[2]),
        pltpu.make_async_copy(skip_in, wsk.at[pl.ds(pl.multiple_of(z * ROWS, 16), ROWS), :], load.at[3]),
        pltpu.make_async_copy(up_in, xs.at[2], load.at[4]),
        pltpu.make_async_copy(bank_in, bank, load.at[5]),
        pltpu.make_async_copy(queue_in, queue, load.at[6]),
    ]
    for copy in loads:
        copy.start()

    barrier = pltpu.get_barrier_semaphore()
    diagonal = {"segment": (s + SEGS + 1 - 2 * y) % SEGS, "ctx": partner}
    greet = [{"ctx": ring_peer(d)} for d in (1, -1, 2, -2, 3, -3, 4)]
    greet += [{"ctx": partner}, {"segment": above}, {"segment": below}, diagonal]
    for peer in greet:
        pl.semaphore_signal(barrier, inc=1, device_id=peer, device_id_type=MESH)

    wo[0, HEAD:HP, :] = jnp.zeros((HP - HEAD, D), BF)
    for block in range(2):
        wqv[block * HP + HEAD : (block + 1) * HP, :] = jnp.zeros((HP - HEAD, D), BF)
    wk[HEAD:128, :] = jnp.zeros((128 - HEAD, D), BF)
    wk[128 + HP : 256, :] = jnp.zeros((128 - HP, D), BF)
    qt[:, :, HP:128, :] = jnp.zeros((2, RING, 128 - HP, 256), BF)

    gain_down, gain_up = gains[0:1, :], gains[1:2, :]
    loads[0].wait()
    act[0, 0] = layer_norm(xs[0].astype(F32), gain_down).astype(BF)
    pl.semaphore_wait(barrier, len(greet))

    def act_ring(t):
        return slot_ring(
            peers, act_send.at[t], act_recv.at[t],
            lambda p, half: act.at[t, p, pl.ds(half * 64, 64), :],
        )

    rings = [act_ring(0), act_ring(1)]
    out_ring = slot_ring(peers, wo_send, wo_recv, lambda p, half: wo.at[p, pl.ds(half * 48, 48), :])
    skip_ring = row_ring(peers, wsk_send, wsk_recv, z, wsk)

    rings[0].begin(0)
    rings[0].begin(1)

    def to_partner(src, dst, send, recv):
        return pltpu.make_async_remote_copy(
            src, dst, send, recv, device_id={"ctx": partner}, device_id_type=MESH
        )

    loads[1].wait()
    wqv[0:HEAD, :] = stage_qkv[0]
    wqv[HP : HP + HEAD, :] = stage_qkv[2]
    wk[0:HEAD, :] = stage_qkv[1]
    w_copies = [
        to_partner(wqv.at[pl.ds(0, 2 * HP), :], wqv.at[pl.ds(2 * HP, 2 * HP), :], w_send.at[0], w_recv.at[0]),
        to_partner(wk.at[pl.ds(0, HP), :], wk.at[pl.ds(128, HP), :], w_send.at[1], w_recv.at[1]),
    ]
    for copy in w_copies:
        copy.start()

    loads[4].wait()
    loads[5].wait()
    skip_first = bank[slots[0, 0]]
    skip_second = bank[slots[1, 0]]
    rising = xs[2]
    operand[0, 0:TOK, :] = jnp.where(y == 0, rising, skip_first)
    give[0] = jnp.where(y == 0, skip_first, rising)
    give[1] = skip_second
    give_copies = [
        to_partner(give.at[t], operand.at[t, pl.ds(TOK, TOK), :], give_ss.at[t], give_rs.at[t])
        for t in range(2)
    ]

    @pl.when(y == 1)
    def _():
        operand[1, 0:TOK, :] = skip_second

    def pair_copies(t, g):
        lo, hi = GROUPS[g]
        n = (hi - lo) * TOK
        return [
            to_partner(
                qs.at[t, pl.ds(lo, hi - lo)],
                qt.at[t, pl.ds(lo, hi - lo), pl.ds(0, HP), pl.ds(128, 128)],
                pair_send.at[t, g, 0], pair_recv.at[t, g, 0],
            ),
            to_partner(
                ks.at[t, pl.ds(lo * TOK, n), :],
                kk.at[t, pl.ds(1024 + lo * TOK, n), :],
                pair_send.at[t, g, 1], pair_recv.at[t, g, 1],
            ),
            to_partner(
                vs.at[t, :, pl.ds(lo * TOK, n)],
                vt.at[t, :, pl.ds(1024 + lo * TOK, n)],
                pair_send.at[t, g, 2], pair_recv.at[t, g, 2],
            ),
        ]

    def project(t, g):
        lo, hi = GROUPS[g]
        n = (hi - lo) * TOK
        tokens = act[t, lo:hi].reshape(n, D)
        made = nt(wqv[...], tokens)
        keys = nt(tokens, wk[...]).astype(BF)
        one = lax.broadcasted_iota(jnp.int32, (HP, n), 0) == HEAD
        own_v = jnp.where(one, 1.0, made[HP : 2 * HP]).astype(BF)
        pair_v = jnp.where(one, 1.0, made[3 * HP : 4 * HP]).astype(BF)
        made = made.astype(BF)
        for p in range(lo, hi):
            cols = slice((p - lo) * TOK, (p - lo + 1) * TOK)
            qt[t, p, 0:HP, 0:128] = made[0:HP, cols]
            qs[t, p] = made[2 * HP : 3 * HP, cols]
        vt[t, :, lo * TOK : hi * TOK] = own_v
        vs[t, :, lo * TOK : hi * TOK] = pair_v
        kk[t, lo * TOK : hi * TOK, :] = keys[:, 0:128]
        ks[t, lo * TOK : hi * TOK, :] = keys[:, 128:256]
        for copy in pair_copies(t, g):
            copy.start()

    def head_copy(t, p, mirror, delta):
        return pltpu.make_async_remote_copy(
            ot.at[t, p], mt.at[t, mirror], head_send.at[t, p], head_recv.at[t, mirror],
            device_id={"ctx": y * 8 + (z + delta + 8) % 8}, device_id_type=MESH,
        )

    def attend_block(t, p):
        queries = qt[t, p]
        peak = None
        for kb in range(8):
            made = jnp.dot(kk[t, kb * 256 : (kb + 1) * 256, :], queries, preferred_element_type=F32)
            scores[kb] = made
            top = jnp.max(made.reshape(32, 8, 256), axis=0)
            peak = top if peak is None else jnp.maximum(peak, top)
        peak = jnp.max(peak, axis=0, keepdims=True)
        total = jnp.zeros((HP, 256), F32)
        for kb in range(8):
            powers = jnp.exp2((scores[kb] - peak) * (SCALE * LOG2E)).astype(BF)
            total += jnp.dot(vt[t, :, kb * 256 : (kb + 1) * 256], powers, preferred_element_type=F32)
        return (total * (1.0 / total[HEAD : HEAD + 1, :])).astype(BF)

    def attend(t, between):
        def body(i, carry):
            p = 7 - i
            ot[t, p] = attend_block(t, p)
            odd = p % 2
            delta = ((p + 1) // 2) * (2 * odd - 1)
            mirror = p + (2 * odd - 1) * (1 - p // 7)

            @pl.when(p > 0)
            def _():
                head_copy(t, p, mirror, delta).start()

            for at, work in between.items():

                @pl.when(i == at)
                def _():
                    work()

            return carry

        lax.fori_loop(0, 8, body, 0)
        mt[t, 0] = ot[t, 0]

    def out_project(t):
        for p in range(1, 8):
            head_copy(t, p, p, 0).wait_recv()
        weights = wo[...].reshape(RING * HP, D)
        heads = mt[t].reshape(RING * HP, 256)
        part_send[t] = tn(heads[:, 128:256], weights).astype(BF)
        copies = [
            to_partner(
                part_send.at[t, pl.ds(h * 64, 64), :], part_recv.at[t, pl.ds(h * 64, 64), :],
                part_ss.at[t, h], part_rs.at[t, h],
            )
            for h in range(2)
        ]
        for copy in copies:
            copy.start()
        own = tn(heads[:, 0:128], weights) + xs[t].astype(F32)
        return own, copies

    def down_copy(h):
        return pltpu.make_async_remote_copy(
            x1.at[0, pl.ds(h * 64, 64), :], down.at[pl.ds(h * 64, 64), :],
            down_ss.at[h], down_rs.at[h], device_id={"segment": above}, device_id_type=MESH,
        )

    def rise_copy():
        return pltpu.make_async_remote_copy(
            asc_out.at[0], operand.at[1, pl.ds(pl.multiple_of(y * TOK, 16), TOK), :],
            rise_ss.at[0], rise_rs.at[y], device_id={"segment": below, "ctx": z}, device_id_type=MESH,
        )

    def turn_copy():
        return pltpu.make_async_remote_copy(
            x1.at[0], operand.at[1, pl.ds(TOK, TOK), :],
            rise_ss.at[1], rise_rs.at[1], device_id={"ctx": partner}, device_id_type=MESH,
        )

    def mix_copy(t):
        return to_partner(asc_send.at[t], asc_recv.at[t], mix_ss.at[t], mix_rs.at[t])

    def ascend_first(t):
        asc_send[t] = jnp.dot(operand[t, TOK : 2 * TOK, :], wsk[...], preferred_element_type=F32).astype(BF)
        mix_copy(t).start()
        return jnp.dot(operand[t, 0:TOK, :], wsk[...], preferred_element_type=F32)

    def ascend_last(t, own):
        mix_copy(t).wait_recv()
        asc_out[t] = layer_norm(own + asc_recv[t].astype(F32), gain_up).astype(BF)
        pltpu.make_async_copy(asc_out.at[t], asc_ref.at[t], store.at[1, t]).start()

    for j in range(7):
        rings[0].step(j)
        if j == 1:
            for copy in w_copies:
                copy.wait_recv()
            project(0, 0)
            project(0, 1)
            give_copies[0].start()
            pl.when(y == 0)(lambda: give_copies[1].start())
        if j == 3:
            project(0, 2)
        if j == 5:
            loads[2].wait()
            out_ring.begin(0)
            out_ring.begin(1)
            project(0, 3)
        if j == 6:
            project(0, 4)
    for g in range(5):
        for copy in pair_copies(0, g):
            copy.wait_recv()
    attend(0, {1: lambda: out_ring.step(0), 3: lambda: out_ring.step(1), 5: lambda: out_ring.step(2), 7: lambda: out_ring.step(3)})
    for j in range(4, 7):
        out_ring.step(j)
    loads[3].wait()
    skip_ring.begin(0)
    skip_ring.begin(1)
    own, copies = out_project(0)
    skip_ring.step(0)
    skip_ring.step(1)
    for h in range(2):
        rows = slice(h * 64, (h + 1) * 64)
        copies[h].wait_recv()
        x1[0, rows, :] = (own[rows] + part_recv[0, rows, :].astype(F32)).astype(BF)
        down_copy(h).start()
    pltpu.make_async_copy(x1.at[0], desc_ref.at[0], store.at[0, 0]).start()

    last = s == SEGS - 1

    @pl.when(jnp.logical_and(last, y == 0))
    def _():
        operand[1, 0:TOK, :] = x1[0]

    @pl.when(jnp.logical_and(last, y == 1))
    def _():
        turn_copy().start()

    loads[6].wait()
    entering = queue[entry[0]]
    for h in range(2):
        rows = slice(h * 64, (h + 1) * 64)
        down_copy(h).wait_recv()
        xs[1, rows, :] = jnp.where(s == 0, entering[rows], down[rows, :])
        act[1, 0, rows, :] = layer_norm(xs[1, rows, :].astype(F32), gain_down).astype(BF)
        rings[1].begin(h)
    project(1, 0)
    skip_ring.step(2)
    skip_ring.step(3)
    for j in range(7):
        rings[1].step(j)
        if j == 1:
            project(1, 1)
            skip_ring.step(4)
        if j == 3:
            project(1, 2)
            skip_ring.step(5)
        if j == 5:
            project(1, 3)
            skip_ring.step(6)
        if j == 6:
            project(1, 4)

    give_copies[0].wait_recv()
    own_up = ascend_first(0)
    for g in range(5):
        for copy in pair_copies(1, g):
            copy.wait_recv()
    ascend_last(0, own_up)

    @pl.when(s > 0)
    def _():
        rise_copy().start()

    attend(1, {})

    own, copies = out_project(1)

    @pl.when(y == 1)
    def _():
        give_copies[1].wait_recv()

    @pl.when(jnp.logical_and(y == 0, s < SEGS - 1))
    def _():
        pltpu.make_async_remote_copy(
            asc_out.at[0], operand.at[1, pl.ds(0, TOK), :], rise_ss.at[0], rise_rs.at[0],
            device_id={"segment": below, "ctx": z}, device_id_type=MESH,
        ).wait_recv()

    @pl.when(y == 0)
    def _():
        turn_copy().wait_recv()

    own_up = ascend_first(1)
    for h in range(2):
        rows = slice(h * 64, (h + 1) * 64)
        copies[h].wait_recv()
        x1[1, rows, :] = (own[rows] + part_recv[1, rows, :].astype(F32)).astype(BF)
    pltpu.make_async_copy(x1.at[1], desc_ref.at[1], store.at[0, 1]).start()
    ascend_last(1, own_up)

    for ring in (*rings, out_ring, skip_ring):
        ring.drain()
    for copy in w_copies:
        copy.wait_send()
    give_copies[0].wait_send()
    pl.when(y == 0)(lambda: give_copies[1].wait_send())
    for t in range(2):
        for g in range(5):
            for copy in pair_copies(t, g):
                copy.wait_send()
        for p in range(1, 8):
            head_copy(t, p, p, 0).wait_send()
        for h in range(2):
            to_partner(
                part_send.at[t, pl.ds(h * 64, 64), :], part_recv.at[t, pl.ds(h * 64, 64), :],
                part_ss.at[t, h], part_rs.at[t, h],
            ).wait_send()
        mix_copy(t).wait_send()
    for h in range(2):
        down_copy(h).wait_send()
    pl.when(s > 0)(lambda: rise_copy().wait_send())
    pl.when(jnp.logical_and(last, y == 1))(lambda: turn_copy().wait_send())
    for t in range(2):
        pltpu.make_async_copy(x1.at[t], desc_ref.at[t], store.at[0, t]).wait()
        pltpu.make_async_copy(asc_out.at[t], asc_ref.at[t], store.at[1, t]).wait()


def on_device(
    carried_down, carried_up, skip_bank, queue, next_entry, skip_slot, w_qkv, w_out, w_skip, gains
):
    hbm = pl.BlockSpec(memory_space=pl.ANY)
    smem = pl.BlockSpec(memory_space=pltpu.SMEM)
    vmem = pl.BlockSpec(memory_space=pltpu.VMEM)
    dma = pltpu.SemaphoreType.DMA
    V = pltpu.VMEM
    scratch = [
        V((3, TOK, D), BF),
        V((TOK, D), BF),
        V((3, TOK, D), BF),
        V((8, TOK, D), BF),
        V((3, HEAD, D), BF),
        V((2, RING, TOK, D), BF),
        V((4 * HP, D), BF),
        V((256, D), BF),
        V((2, RING, 128, 256), BF),
        V((2, 2048, 128), BF),
        V((2, HP, 2048), BF),
        V((2, RING, HP, 128), BF),
        V((2, 1024, 128), BF),
        V((2, HP, 1024), BF),
        V((8, 256, 256), F32),
        V((2, RING, HP, 256), BF),
        V((2, RING, HP, 256), BF),
        V((RING, HP, D), BF),
        V((D, D), BF),
        V((2, TOK, D), BF),
        V((2, TOK, D), BF),
        V((2, TOK, D), BF),
        V((2, 2 * TOK, D), BF),
        V((2, TOK, D), BF),
        V((2, TOK, D), BF),
        V((2, TOK, D), BF),
        V((2, TOK, D), BF),
        dma((7,)), dma((2, 2)),
        dma((2, 2, 7)), dma((2, 2, 7)), dma((2, 7)), dma((2, 7)), dma((2, 7)), dma((2, 7)),
        dma((2, 5, 3)), dma((2, 5, 3)), dma((2,)), dma((2,)), dma((2, 8)), dma((2, 8)),
        dma((2, 2)), dma((2, 2)), dma((2,)), dma((2,)), dma((2,)), dma((2,)),
        dma((2,)), dma((2,)), dma((2,)), dma((2,)),
    ]
    desc, asc = pl.pallas_call(
        kernel,
        out_shape=(
            jax.ShapeDtypeStruct((2, TOK, D), BF),
            jax.ShapeDtypeStruct((2, TOK, D), BF),
        ),
        in_specs=[hbm, hbm, hbm, hbm, smem, smem, hbm, hbm, hbm, vmem],
        out_specs=(hbm, hbm),
        scratch_shapes=scratch,
        compiler_params=pltpu.CompilerParams(
            collective_id=0, has_side_effects=True, vmem_limit_bytes=60 * 1024 * 1024
        ),
    )(
        carried_down[0], carried_up[0], skip_bank[0], queue, next_entry, skip_slot,
        w_qkv[0], w_out[0], w_skip[0], gains[0],
    )
    return desc[:, None], asc[:, None]


def solution(mesh):
    in_specs = (
        P("segment", "ctx", None),
        P("segment", "ctx", None),
        P("segment", None, "ctx", None),
        P(None, "ctx", None),
        P(),
        P(None, "segment"),
        P("segment", None, "ctx", None),
        P("segment", "ctx", None),
        P("segment", "ctx", None),
        P("segment", None, None),
    )
    out_specs = (P(None, "segment", "ctx", None), P(None, "segment", "ctx", None))
    return jax.shard_map(
        on_device, mesh=mesh, in_specs=in_specs, out_specs=out_specs, check_vma=False
    )
```

```python
import jax
import jax.numpy as jnp
from jax import lax
from jax.experimental import pallas as pl
from jax.experimental.pallas import tpu as pltpu
from jax.sharding import PartitionSpec as P

HEAD = 88
HP = 96
D = 1408
TOK = 128
RING = 8
SEGS = 16
ROWS = 176
SCALE = HEAD**-0.5
LOG2E = 1.4426950408889634
MESH = pl.DeviceIdType.MESH
BF = jnp.bfloat16
F32 = jnp.float32
GROUPS = ((0, 1), (1, 3), (3, 5), (5, 7), (7, 8))


def slot_of(delta):
    if delta == 0:
        return 0
    if abs(delta) == 4:
        return 7
    return 2 * delta - 1 if delta > 0 else -2 * delta


def nt(a, b):
    return lax.dot_general(a, b, (((1,), (1,)), ((), ())), preferred_element_type=F32)


def tn(a, b):
    return lax.dot_general(a, b, (((0,), (0,)), ((), ())), preferred_element_type=F32)


def layer_norm(x, gain):
    center = x - jnp.mean(x, axis=-1, keepdims=True)
    spread = jnp.mean(center * center, axis=-1, keepdims=True)
    return center * lax.rsqrt(spread + 1e-06) * gain


class Ring:
    def __init__(self, peers, send, recv, src, dst):
        self.peers, self.send, self.recv, self.src, self.dst = peers, send, recv, src, dst

    def copy(self, way, j):
        hops, half = j // 2, (way if j == 6 else j % 2)
        return pltpu.make_async_remote_copy(
            self.src(way, hops, half),
            self.dst(way, hops, half),
            self.send.at[way, j],
            self.recv.at[way, j],
            device_id={"ctx": self.peers[way]},
            device_id_type=MESH,
        )

    def start(self, way, j):
        self.copy(way, j).start()

    def arrive(self, way, j):
        hops, half = j // 2, (way if j == 6 else j % 2)
        here = self.src(way, hops + 1, half)
        pltpu.make_async_remote_copy(
            here,
            here,
            self.send.at[way, j],
            self.recv.at[way, j],
            device_id={"ctx": self.peers[way]},
            device_id_type=MESH,
        ).wait_recv()

    def begin(self, half):
        self.start(0, half)
        self.start(1, half)

    def step(self, j):
        for way in (0, 1):
            self.arrive(way, j)
            if j < 4:
                self.start(way, j + 2)
            elif j == 4 + way:
                self.start(way, 6)

    def drain(self):
        for way in (0, 1):
            for j in range(7):
                self.copy(way, j).wait_send()


def slot_ring(peers, send, recv, view):
    def src(way, hops, half):
        return view(slot_of(-hops if way == 0 else hops), half)

    def dst(way, hops, half):
        return view(slot_of(-hops - 1 if way == 0 else hops + 1), half)

    return Ring(peers, send, recv, src, dst)


def row_ring(peers, send, recv, z, buf):
    def src(way, hops, half):
        origin = lax.rem(z + (8 - hops if way == 0 else hops), 8)
        start = pl.multiple_of(origin * ROWS + half * 96, 16)
        return buf.at[pl.ds(start, 80 if half else 96), :]

    return Ring(peers, send, recv, src, src)


def kernel(
    x_in, up_in, bank_in, queue_in, entry, slots, qkv_in, out_in, skip_in, gains,
    desc_ref, asc_ref,
    xs, down, bank, queue, stage_qkv, act, wqv, wk, qt, kk, vt, qs, ks, vs, scores, ot, mt,
    wo, wsk, part_send, part_recv, x1, operand, give, asc_send, asc_recv, asc_out, own_up,
    load, store, act_send, act_recv, wo_send, wo_recv, wsk_send, wsk_recv,
    pair_send, pair_recv, w_send, w_recv, head_send, head_recv,
    part_ss, part_rs, down_ss, down_rs, give_ss, give_rs, rise_ss, rise_rs, mix_ss, mix_rs,
):
    s = lax.axis_index("segment")
    c = lax.axis_index("ctx")
    y, z = c // 8, c % 8
    partner = (1 - y) * 8 + z
    above, below = (s + 1) % SEGS, (s + SEGS - 1) % SEGS

    def ring_peer(delta):
        return y * 8 + (z + delta + 8) % 8

    peers = (ring_peer(1), ring_peer(-1))

    loads = [
        pltpu.make_async_copy(x_in, xs.at[0], load.at[0]),
        pltpu.make_async_copy(qkv_in, stage_qkv, load.at[1]),
        pltpu.make_async_copy(out_in, wo.at[0, pl.ds(0, HEAD), :], load.at[2]),
        pltpu.make_async_copy(skip_in, wsk.at[pl.ds(pl.multiple_of(z * ROWS, 16), ROWS), :], load.at[3]),
        pltpu.make_async_copy(up_in, xs.at[2], load.at[4]),
        pltpu.make_async_copy(bank_in, bank, load.at[5]),
        pltpu.make_async_copy(queue_in, queue, load.at[6]),
    ]
    for copy in loads:
        copy.start()

    barrier = pltpu.get_barrier_semaphore()
    diagonal = {"segment": (s + SEGS + 1 - 2 * y) % SEGS, "ctx": partner}
    greet = [{"ctx": ring_peer(d)} for d in (1, -1, 2, -2, 3, -3, 4)]
    greet += [{"ctx": partner}, {"segment": above}, {"segment": below}, diagonal]
    for peer in greet:
        pl.semaphore_signal(barrier, inc=1, device_id=peer, device_id_type=MESH)

    pad = HP - HEAD
    wo[:, HEAD:HP, :] = jnp.zeros((RING, pad, D), BF)
    for block in range(4):
        wqv[block * HP + HEAD : (block + 1) * HP, :] = jnp.zeros((pad, D), BF)
    for block in range(2):
        wk[block * 128 + HEAD : (block + 1) * 128, :] = jnp.zeros((128 - HEAD, D), BF)
    qt[:, :, HEAD:128, :] = jnp.zeros((2, 2, 128 - HEAD, 1024), BF)
    mt[:, :, :, HEAD:HP, :] = jnp.zeros((2, 2, RING, pad, TOK), BF)
    ones = (lax.broadcasted_iota(jnp.int32, (pad, 2048), 0) == 0).astype(F32).astype(BF)
    for t in range(2):
        vt[t, HEAD:HP, :] = ones

    gain_down, gain_up = gains[0:1, :], gains[1:2, :]
    loads[0].wait()
    act[0, 0] = layer_norm(xs[0].astype(F32), gain_down).astype(BF)
    loads[1].wait()
    wqv[0:HEAD, :] = stage_qkv[0]
    wqv[HP : HP + HEAD, :] = stage_qkv[2]
    wk[0:HEAD, :] = stage_qkv[1]
    loads[4].wait()
    loads[5].wait()
    skip_first = bank[slots[0, 0]]
    skip_second = bank[slots[0, 1]]
    rising = xs[2]
    operand[0, 0:TOK, :] = jnp.where(y == 0, rising, skip_first)
    give[0] = jnp.where(y == 0, skip_first, rising)
    give[1] = skip_second

    @pl.when(y == 1)
    def _():
        operand[1, 0:TOK, :] = skip_second

    def act_ring(t):
        return slot_ring(
            peers, act_send.at[t], act_recv.at[t],
            lambda p, half: act.at[t, p, pl.ds(half * 64, 64), :],
        )

    rings = [act_ring(0), act_ring(1)]
    out_ring = slot_ring(peers, wo_send, wo_recv, lambda p, half: wo.at[p, pl.ds(half * 48, 40 if half else 48), :])
    skip_ring = row_ring(peers, wsk_send, wsk_recv, z, wsk)

    def to_partner(src, dst, send, recv):
        return pltpu.make_async_remote_copy(
            src, dst, send, recv, device_id={"ctx": partner}, device_id_type=MESH
        )

    w_copies = [
        to_partner(wqv.at[pl.ds(0, HEAD), :], wqv.at[pl.ds(2 * HP, HEAD), :], w_send.at[0], w_recv.at[0]),
        to_partner(wqv.at[pl.ds(HP, HEAD), :], wqv.at[pl.ds(3 * HP, HEAD), :], w_send.at[1], w_recv.at[1]),
        to_partner(wk.at[pl.ds(0, HEAD), :], wk.at[pl.ds(128, HEAD), :], w_send.at[2], w_recv.at[2]),
    ]
    give_copies = [
        to_partner(give.at[t], operand.at[t, pl.ds(TOK, TOK), :], give_ss.at[t], give_rs.at[t])
        for t in range(2)
    ]

    pl.semaphore_wait(barrier, len(greet))
    rings[0].begin(0)
    rings[0].begin(1)
    for copy in w_copies:
        copy.start()

    def pair_copies(t, g):
        lo, hi = GROUPS[g]
        n = (hi - lo) * TOK
        return [
            to_partner(
                qs.at[t, :, pl.ds(lo * TOK, n)],
                qt.at[t, 1, pl.ds(0, HEAD), pl.ds(lo * TOK, n)],
                pair_send.at[t, g, 0], pair_recv.at[t, g, 0],
            ),
            to_partner(
                ks.at[t, pl.ds(lo * TOK, n), :],
                kk.at[t, pl.ds(1024 + lo * TOK, n), :],
                pair_send.at[t, g, 1], pair_recv.at[t, g, 1],
            ),
            to_partner(
                vs.at[t, :, pl.ds(lo * TOK, n)],
                vt.at[t, pl.ds(0, HEAD), pl.ds(1024 + lo * TOK, n)],
                pair_send.at[t, g, 2], pair_recv.at[t, g, 2],
            ),
        ]

    def project(t, g):
        lo, hi = GROUPS[g]
        n = (hi - lo) * TOK
        tokens = act[t, lo:hi].reshape(n, D)
        made = nt(wqv[...], tokens)
        keys = nt(tokens, wk[...]).astype(BF)
        made = made.astype(BF)
        qt[t, 0, 0:HEAD, lo * TOK : hi * TOK] = made[0:HEAD]
        vt[t, 0:HEAD, lo * TOK : hi * TOK] = made[HP : HP + HEAD]
        qs[t, :, lo * TOK : hi * TOK] = made[2 * HP : 2 * HP + HEAD]
        vs[t, :, lo * TOK : hi * TOK] = made[3 * HP : 3 * HP + HEAD]
        kk[t, lo * TOK : hi * TOK, :] = keys[:, 0:128]
        ks[t, lo * TOK : hi * TOK, :] = keys[:, 128:256]
        for copy in pair_copies(t, g):
            copy.start()

    def head_copy(t, half, p, mirror, delta):
        return pltpu.make_async_remote_copy(
            ot.at[t, half, p], mt.at[t, half, mirror, pl.ds(0, HEAD), :],
            head_send.at[t, half, p], head_recv.at[t, half, mirror],
            device_id={"ctx": y * 8 + (z + delta + 8) % 8}, device_id_type=MESH,
        )

    def attend_block(t, half, b):
        queries = qt[t, half, :, pl.ds(pl.multiple_of(b * 256, 256), 256)]
        peak = None
        for kb in range(8):
            made = jnp.dot(kk[t, kb * 256 : (kb + 1) * 256, :], queries, preferred_element_type=F32)
            scores[kb] = made
            top = jnp.max(made.reshape(32, 8, 256), axis=0)
            peak = top if peak is None else jnp.maximum(peak, top)
        peak = jnp.max(peak, axis=0, keepdims=True)
        total = jnp.zeros((HP, 256), F32)
        for kb in range(8):
            powers = jnp.exp2((scores[kb] - peak) * (SCALE * LOG2E)).astype(BF)
            total += jnp.dot(vt[t, :, kb * 256 : (kb + 1) * 256], powers, preferred_element_type=F32)
        return (total[0:HEAD] * (1.0 / total[HEAD : HEAD + 1, :])).astype(BF)

    def attend(t, half, first, stop, between):
        def body(i, carry):
            b = 3 - i
            made = attend_block(t, half, b)
            ot[t, half, 2 * b + 1] = made[:, TOK : 2 * TOK]
            ot[t, half, 2 * b] = made[:, 0:TOK]
            head_copy(t, half, 2 * b + 1, 2 * b + 2 - b // 3, b + 1).start()

            @pl.when(b > 0)
            def _():
                head_copy(t, half, 2 * b, 2 * b - 1, -b).start()

            for at, work in between.items():

                @pl.when(i == at)
                def _():
                    work()

            return carry

        lax.fori_loop(first, stop, body, 0)
        if stop == 4:
            mt[t, half, 0, 0:HEAD, :] = ot[t, half, 0]

    def part_copy(t, h):
        return to_partner(
            part_send.at[t, pl.ds(h * 64, 64), :], part_recv.at[t, pl.ds(h * 64, 64), :],
            part_ss.at[t, h], part_rs.at[t, h],
        )

    def heads_times_out(t, half):
        for p in range(1, 8):
            head_copy(t, half, p, p, 1).wait_recv()
        weights = wo[...].reshape(RING * HP, D)
        return tn(mt[t, half].reshape(RING * HP, TOK), weights)

    def project_pair(t):
        part_send[t] = heads_times_out(t, 1).astype(BF)
        for h in range(2):
            part_copy(t, h).start()

    def project_own(t):
        return heads_times_out(t, 0) + xs[t].astype(F32)

    def finish(t, h, own):
        rows = slice(h * 64, (h + 1) * 64)
        part_copy(t, h).wait_recv()
        x1[t, rows, :] = (own[rows] + part_recv[t, rows, :].astype(F32)).astype(BF)

    def down_copy(h):
        return pltpu.make_async_remote_copy(
            x1.at[0, pl.ds(h * 64, 64), :], down.at[pl.ds(h * 64, 64), :],
            down_ss.at[h], down_rs.at[h], device_id={"segment": above}, device_id_type=MESH,
        )

    def rise_copy():
        return pltpu.make_async_remote_copy(
            asc_out.at[0], operand.at[1, pl.ds(pl.multiple_of(y * TOK, 16), TOK), :],
            rise_ss.at[0], rise_rs.at[y], device_id={"segment": below, "ctx": z}, device_id_type=MESH,
        )

    def turn_copy():
        return pltpu.make_async_remote_copy(
            x1.at[0], operand.at[1, pl.ds(TOK, TOK), :],
            rise_ss.at[1], rise_rs.at[1], device_id={"ctx": partner}, device_id_type=MESH,
        )

    def mix_copy(t):
        return to_partner(asc_send.at[t], asc_recv.at[t], mix_ss.at[t], mix_rs.at[t])

    def ascend_first(t):
        asc_send[t] = jnp.dot(operand[t, TOK : 2 * TOK, :], wsk[...], preferred_element_type=F32).astype(BF)
        own_up[...] = jnp.dot(operand[t, 0:TOK, :], wsk[...], preferred_element_type=F32)

    def ascend_last(t):
        mix_copy(t).wait_recv()
        asc_out[t] = layer_norm(own_up[...] + asc_recv[t].astype(F32), gain_up).astype(BF)
        pltpu.make_async_copy(asc_out.at[t], asc_ref.at[t], store.at[1, t]).start()

    for j in range(4):
        rings[0].step(j)
    for copy in w_copies:
        copy.wait_recv()
    for g in range(3):
        project(0, g)
    rings[0].step(4)
    rings[0].step(5)
    loads[2].wait()
    out_ring.begin(0)
    project(0, 3)
    rings[0].step(6)
    out_ring.begin(1)
    project(0, 4)
    for g in range(5):
        for copy in pair_copies(0, g):
            copy.wait_recv()
    give_copies[0].start()
    pl.when(y == 0)(lambda: give_copies[1].start())
    attend(0, 1, 0, 4, {1: lambda: out_ring.step(0), 3: lambda: out_ring.step(1)})
    attend(0, 0, 0, 4, {1: lambda: out_ring.step(2), 3: lambda: out_ring.step(3)})
    loads[3].wait()
    out_ring.step(4)
    out_ring.step(5)
    skip_ring.begin(0)
    out_ring.step(6)
    skip_ring.begin(1)
    project_pair(0)
    own = project_own(0)
    skip_ring.step(0)
    skip_ring.step(1)
    for h in range(2):
        finish(0, h, own)
        down_copy(h).start()
    pltpu.make_async_copy(x1.at[0], desc_ref.at[0], store.at[0, 0]).start()

    last = s == SEGS - 1

    @pl.when(jnp.logical_and(last, y == 0))
    def _():
        operand[1, 0:TOK, :] = x1[0]

    @pl.when(jnp.logical_and(last, y == 1))
    def _():
        turn_copy().start()

    skip_ring.step(2)
    skip_ring.step(3)
    loads[6].wait()
    entering = queue[entry[0]]
    for h in range(2):
        rows = slice(h * 64, (h + 1) * 64)
        down_copy(h).wait_recv()
        xs[1, rows, :] = jnp.where(s == 0, entering[rows], down[rows, :])
        act[1, 0, rows, :] = layer_norm(xs[1, rows, :].astype(F32), gain_down).astype(BF)
    project(1, 0)
    skip_ring.step(4)
    rings[1].begin(0)
    skip_ring.step(5)
    rings[1].begin(1)
    skip_ring.step(6)

    give_copies[0].wait_recv()
    ascend_first(0)
    mix_copy(0).start()
    rings[1].step(0)
    rings[1].step(1)
    project(1, 1)
    ascend_last(0)
    pl.when(s > 0)(lambda: rise_copy().start())
    rings[1].step(2)
    rings[1].step(3)
    project(1, 2)

    @pl.when(y == 1)
    def _():
        give_copies[1].wait_recv()
        ascend_first(1)

    rings[1].step(4)
    rings[1].step(5)
    project(1, 3)

    @pl.when(jnp.logical_and(y == 0, s < SEGS - 1))
    def _():
        pltpu.make_async_remote_copy(
            asc_out.at[0], operand.at[1, pl.ds(0, TOK), :], rise_ss.at[0], rise_rs.at[0],
            device_id={"segment": below, "ctx": z}, device_id_type=MESH,
        ).wait_recv()

    @pl.when(y == 0)
    def _():
        turn_copy().wait_recv()
        ascend_first(1)

    rings[1].step(6)
    project(1, 4)
    for g in range(5):
        for copy in pair_copies(1, g):
            copy.wait_recv()
    mix_copy(1).start()
    attend(1, 1, 0, 4, {})
    attend(1, 0, 0, 2, {})
    project_pair(1)
    attend(1, 0, 2, 4, {})
    ascend_last(1)
    own = project_own(1)
    for h in range(2):
        finish(1, h, own)
    pltpu.make_async_copy(x1.at[1], desc_ref.at[1], store.at[0, 1]).start()

    for ring in (*rings, out_ring, skip_ring):
        ring.drain()
    for copy in w_copies:
        copy.wait_send()
    give_copies[0].wait_send()
    pl.when(y == 0)(lambda: give_copies[1].wait_send())
    for t in range(2):
        for g in range(5):
            for copy in pair_copies(t, g):
                copy.wait_send()
        mix_copy(t).wait_send()
        for half in range(2):
            for p in range(1, 8):
                head_copy(t, half, p, p, 1).wait_send()
        for h in range(2):
            part_copy(t, h).wait_send()
    for h in range(2):
        down_copy(h).wait_send()
    pl.when(s > 0)(lambda: rise_copy().wait_send())
    pl.when(jnp.logical_and(last, y == 1))(lambda: turn_copy().wait_send())
    for t in range(2):
        pltpu.make_async_copy(x1.at[t], desc_ref.at[t], store.at[0, t]).wait()
        pltpu.make_async_copy(asc_out.at[t], asc_ref.at[t], store.at[1, t]).wait()


def on_device(
    carried_down, carried_up, skip_bank, queue, next_entry, skip_slot, w_qkv, w_out, w_skip, gains
):
    hbm = pl.BlockSpec(memory_space=pl.ANY)
    smem = pl.BlockSpec(memory_space=pltpu.SMEM)
    vmem = pl.BlockSpec(memory_space=pltpu.VMEM)
    dma = pltpu.SemaphoreType.DMA
    V = pltpu.VMEM
    scratch = [
        V((3, TOK, D), BF),
        V((TOK, D), BF),
        V((3, TOK, D), BF),
        V((8, TOK, D), BF),
        V((3, HEAD, D), BF),
        V((2, RING, TOK, D), BF),
        V((4 * HP, D), BF),
        V((256, D), BF),
        V((2, 2, 128, 1024), BF),
        V((2, 2048, 128), BF),
        V((2, HP, 2048), BF),
        V((2, HEAD, 1024), BF),
        V((2, 1024, 128), BF),
        V((2, HEAD, 1024), BF),
        V((8, 256, 256), F32),
        V((2, 2, RING, HEAD, TOK), BF),
        V((2, 2, RING, HP, TOK), BF),
        V((RING, HP, D), BF),
        V((D, D), BF),
        V((2, TOK, D), BF),
        V((2, TOK, D), BF),
        V((2, TOK, D), BF),
        V((2, 2 * TOK, D), BF),
        V((2, TOK, D), BF),
        V((2, TOK, D), BF),
        V((2, TOK, D), BF),
        V((2, TOK, D), BF),
        V((TOK, D), F32),
        dma((7,)), dma((2, 2)),
        dma((2, 2, 7)), dma((2, 2, 7)), dma((2, 7)), dma((2, 7)), dma((2, 7)), dma((2, 7)),
        dma((2, 5, 3)), dma((2, 5, 3)), dma((3,)), dma((3,)), dma((2, 2, 8)), dma((2, 2, 8)),
        dma((2, 2)), dma((2, 2)), dma((2,)), dma((2,)), dma((2,)), dma((2,)),
        dma((2,)), dma((2,)), dma((2,)), dma((2,)),
    ]
    desc, asc = pl.pallas_call(
        kernel,
        out_shape=(
            jax.ShapeDtypeStruct((2, TOK, D), BF),
            jax.ShapeDtypeStruct((2, TOK, D), BF),
        ),
        in_specs=[hbm, hbm, hbm, hbm, smem, smem, hbm, hbm, hbm, vmem],
        out_specs=(hbm, hbm),
        scratch_shapes=scratch,
        compiler_params=pltpu.CompilerParams(
            collective_id=0, has_side_effects=True, vmem_limit_bytes=60 * 1024 * 1024
        ),
    )(
        carried_down[0], carried_up[0], skip_bank[0], queue, next_entry, skip_slot.T,
        w_qkv[0], w_out[0], w_skip[0], gains[0],
    )
    return desc[:, None], asc[:, None]


def solution(mesh):
    in_specs = (
        P("segment", "ctx", None),
        P("segment", "ctx", None),
        P("segment", None, "ctx", None),
        P(None, "ctx", None),
        P(),
        P(None, "segment"),
        P("segment", None, "ctx", None),
        P("segment", "ctx", None),
        P("segment", "ctx", None),
        P("segment", None, None),
    )
    out_specs = (P(None, "segment", "ctx", None), P(None, "segment", "ctx", None))
    return jax.shard_map(
        on_device, mesh=mesh, in_specs=in_specs, out_specs=out_specs, check_vma=False
    )
```

```python
import jax
import jax.numpy as jnp
from jax import lax
from jax.experimental import pallas as pl
from jax.experimental.pallas import tpu as pltpu
from jax.sharding import PartitionSpec as P

HEAD = 88
HP = 96
D = 1408
TOK = 128
RING = 8
SEGS = 16
ROWS = 176
SCALE = HEAD**-0.5
LOG2E = 1.4426950408889634
MESH = pl.DeviceIdType.MESH
BF = jnp.bfloat16
F32 = jnp.float32
GROUPS = ((0, 1), (1, 3), (3, 5), (5, 7), (7, 8))


def slot_of(delta):
    if delta == 0:
        return 0
    if abs(delta) == 4:
        return 7
    return 2 * delta - 1 if delta > 0 else -2 * delta


def nt(a, b):
    return lax.dot_general(a, b, (((1,), (1,)), ((), ())), preferred_element_type=F32)


def tn(a, b):
    return lax.dot_general(a, b, (((0,), (0,)), ((), ())), preferred_element_type=F32)


def layer_norm(x, gain):
    center = x - jnp.mean(x, axis=-1, keepdims=True)
    spread = jnp.mean(center * center, axis=-1, keepdims=True)
    return center * lax.rsqrt(spread + 1e-06) * gain


class Ring:
    def __init__(self, peers, send, recv, src, dst):
        self.peers, self.send, self.recv, self.src, self.dst = peers, send, recv, src, dst

    def copy(self, way, j):
        hops, half = j // 2, (way if j == 6 else j % 2)
        return pltpu.make_async_remote_copy(
            self.src(way, hops, half),
            self.dst(way, hops, half),
            self.send.at[way, j],
            self.recv.at[way, j],
            device_id={"ctx": self.peers[way]},
            device_id_type=MESH,
        )

    def start(self, way, j):
        self.copy(way, j).start()

    def arrive(self, way, j):
        hops, half = j // 2, (way if j == 6 else j % 2)
        here = self.src(way, hops + 1, half)
        pltpu.make_async_remote_copy(
            here,
            here,
            self.send.at[way, j],
            self.recv.at[way, j],
            device_id={"ctx": self.peers[way]},
            device_id_type=MESH,
        ).wait_recv()

    def begin(self, half):
        self.start(0, half)
        self.start(1, half)

    def step(self, j):
        for way in (0, 1):
            self.arrive(way, j)
            if j < 4:
                self.start(way, j + 2)
            elif j == 4 + way:
                self.start(way, 6)

    def drain(self):
        for way in (0, 1):
            for j in range(7):
                self.copy(way, j).wait_send()


def slot_ring(peers, send, recv, view):
    def src(way, hops, half):
        return view(slot_of(-hops if way == 0 else hops), half)

    def dst(way, hops, half):
        return view(slot_of(-hops - 1 if way == 0 else hops + 1), half)

    return Ring(peers, send, recv, src, dst)


def row_ring(peers, send, recv, z, buf):
    def src(way, hops, half):
        origin = lax.rem(z + (8 - hops if way == 0 else hops), 8)
        start = pl.multiple_of(origin * ROWS + half * 96, 16)
        return buf.at[pl.ds(start, 80 if half else 96), :]

    return Ring(peers, send, recv, src, src)


def kernel(
    x_in, up_in, bank_in, queue_in, entry, slots, qkv_in, out_in, skip_in, gains,
    desc_ref, asc_ref,
    xs, down, bank, queue, stage_qkv, act, wqv, wk, qt, kk, vt, qs, ks, vs, scores, ot, mt,
    wo, wsk, part_send, part_recv, x1, operand, give, asc_send, asc_recv, asc_out, own_up,
    load, store, act_send, act_recv, wo_send, wo_recv, wsk_send, wsk_recv,
    pair_send, pair_recv, w_send, w_recv, head_send, head_recv,
    part_ss, part_rs, down_ss, down_rs, give_ss, give_rs, rise_ss, rise_rs, mix_ss, mix_rs,
):
    s = lax.axis_index("segment")
    c = lax.axis_index("ctx")
    y, z = c // 8, c % 8
    partner = (1 - y) * 8 + z
    above, below = (s + 1) % SEGS, (s + SEGS - 1) % SEGS

    def ring_peer(delta):
        return y * 8 + (z + delta + 8) % 8

    peers = (ring_peer(1), ring_peer(-1))

    loads = [
        pltpu.make_async_copy(x_in, xs.at[0], load.at[0]),
        pltpu.make_async_copy(qkv_in, stage_qkv, load.at[1]),
        pltpu.make_async_copy(out_in, wo.at[0, pl.ds(0, HEAD), :], load.at[2]),
        pltpu.make_async_copy(skip_in, wsk.at[pl.ds(pl.multiple_of(z * ROWS, 16), ROWS), :], load.at[3]),
        pltpu.make_async_copy(up_in, xs.at[2], load.at[4]),
        pltpu.make_async_copy(bank_in, bank, load.at[5]),
        pltpu.make_async_copy(queue_in, queue, load.at[6]),
    ]
    for copy in loads:
        copy.start()

    barrier = pltpu.get_barrier_semaphore()
    diagonal = {"segment": (s + SEGS + 1 - 2 * y) % SEGS, "ctx": partner}
    greet = [{"ctx": ring_peer(d)} for d in (1, -1, 2, -2, 3, -3, 4)]
    greet += [{"ctx": partner}, {"segment": above}, {"segment": below}, diagonal]
    for peer in greet:
        pl.semaphore_signal(barrier, inc=1, device_id=peer, device_id_type=MESH)

    pad = HP - HEAD
    wo[:, HEAD:HP, :] = jnp.zeros((RING, pad, D), BF)
    for block in range(4):
        wqv[block * HP + HEAD : (block + 1) * HP, :] = jnp.zeros((pad, D), BF)
    for block in range(2):
        wk[block * 128 + HEAD : (block + 1) * 128, :] = jnp.zeros((128 - HEAD, D), BF)
    qt[:, :, HEAD:128, :] = jnp.zeros((2, 2, 128 - HEAD, 1024), BF)
    mt[:, :, :, HEAD:HP, :] = jnp.zeros((2, 2, RING, pad, TOK), BF)
    ones = (lax.broadcasted_iota(jnp.int32, (pad, 2048), 0) == 0).astype(F32).astype(BF)
    for t in range(2):
        vt[t, HEAD:HP, :] = ones

    gain_down, gain_up = gains[0:1, :], gains[1:2, :]
    loads[0].wait()
    act[0, 0] = layer_norm(xs[0].astype(F32), gain_down).astype(BF)
    loads[1].wait()
    wqv[0:HEAD, :] = stage_qkv[0]
    wqv[HP : HP + HEAD, :] = stage_qkv[2]
    wk[0:HEAD, :] = stage_qkv[1]
    loads[4].wait()
    loads[5].wait()
    skip_first = bank[slots[0, 0]]
    skip_second = bank[slots[0, 1]]
    rising = xs[2]
    operand[0, 0:TOK, :] = jnp.where(y == 0, rising, skip_first)
    give[0] = jnp.where(y == 0, skip_first, rising)
    give[1] = skip_second

    @pl.when(y == 1)
    def _():
        operand[1, 0:TOK, :] = skip_second

    def act_ring(t):
        return slot_ring(
            peers, act_send.at[t], act_recv.at[t],
            lambda p, half: act.at[t, p, pl.ds(half * 64, 64), :],
        )

    rings = [act_ring(0), act_ring(1)]
    out_ring = slot_ring(peers, wo_send, wo_recv, lambda p, half: wo.at[p, pl.ds(half * 48, 40 if half else 48), :])
    skip_ring = row_ring(peers, wsk_send, wsk_recv, z, wsk)

    def to_partner(src, dst, send, recv):
        return pltpu.make_async_remote_copy(
            src, dst, send, recv, device_id={"ctx": partner}, device_id_type=MESH
        )

    w_copies = [
        to_partner(wqv.at[pl.ds(0, HEAD), :], wqv.at[pl.ds(2 * HP, HEAD), :], w_send.at[0], w_recv.at[0]),
        to_partner(wqv.at[pl.ds(HP, HEAD), :], wqv.at[pl.ds(3 * HP, HEAD), :], w_send.at[1], w_recv.at[1]),
        to_partner(wk.at[pl.ds(0, HEAD), :], wk.at[pl.ds(128, HEAD), :], w_send.at[2], w_recv.at[2]),
    ]
    give_copies = [
        to_partner(give.at[t], operand.at[t, pl.ds(TOK, TOK), :], give_ss.at[t], give_rs.at[t])
        for t in range(2)
    ]

    pl.semaphore_wait(barrier, len(greet))
    rings[0].begin(0)
    rings[0].begin(1)
    for copy in w_copies:
        copy.start()

    def pair_copies(t, g):
        lo, hi = GROUPS[g]
        n = (hi - lo) * TOK
        return [
            to_partner(
                qs.at[t, :, pl.ds(lo * TOK, n)],
                qt.at[t, 1, pl.ds(0, HEAD), pl.ds(lo * TOK, n)],
                pair_send.at[t, g, 0], pair_recv.at[t, g, 0],
            ),
            to_partner(
                ks.at[t, pl.ds(lo * TOK, n), :],
                kk.at[t, pl.ds(1024 + lo * TOK, n), :],
                pair_send.at[t, g, 1], pair_recv.at[t, g, 1],
            ),
            to_partner(
                vs.at[t, :, pl.ds(lo * TOK, n)],
                vt.at[t, pl.ds(0, HEAD), pl.ds(1024 + lo * TOK, n)],
                pair_send.at[t, g, 2], pair_recv.at[t, g, 2],
            ),
        ]

    def project(t, g):
        lo, hi = GROUPS[g]
        n = (hi - lo) * TOK
        tokens = act[t, lo:hi].reshape(n, D)
        made = nt(wqv[...], tokens)
        keys = nt(tokens, wk[...]).astype(BF)
        made = made.astype(BF)
        qt[t, 0, 0:HEAD, lo * TOK : hi * TOK] = made[0:HEAD]
        vt[t, 0:HEAD, lo * TOK : hi * TOK] = made[HP : HP + HEAD]
        qs[t, :, lo * TOK : hi * TOK] = made[2 * HP : 2 * HP + HEAD]
        vs[t, :, lo * TOK : hi * TOK] = made[3 * HP : 3 * HP + HEAD]
        kk[t, lo * TOK : hi * TOK, :] = keys[:, 0:128]
        ks[t, lo * TOK : hi * TOK, :] = keys[:, 128:256]
        for copy in pair_copies(t, g):
            copy.start()

    def head_copy(t, half, p, mirror, delta):
        return pltpu.make_async_remote_copy(
            ot.at[t, half, p], mt.at[t, half, mirror, pl.ds(0, HEAD), :],
            head_send.at[t, half, p], head_recv.at[t, half, mirror],
            device_id={"ctx": y * 8 + (z + delta + 8) % 8}, device_id_type=MESH,
        )

    def attend_block(t, half, b):
        queries = qt[t, half, :, pl.ds(pl.multiple_of(b * 256, 256), 256)]
        peak = None
        for kb in range(8):
            made = jnp.dot(kk[t, kb * 256 : (kb + 1) * 256, :], queries, preferred_element_type=F32)
            scores[kb] = made
            top = jnp.max(made.reshape(32, 8, 256), axis=0)
            peak = top if peak is None else jnp.maximum(peak, top)
        peak = jnp.max(peak, axis=0, keepdims=True)
        total = jnp.zeros((HP, 256), F32)
        for kb in range(8):
            powers = jnp.exp2((scores[kb] - peak) * (SCALE * LOG2E)).astype(BF)
            total += jnp.dot(vt[t, :, kb * 256 : (kb + 1) * 256], powers, preferred_element_type=F32)
        return (total[0:HEAD] * (1.0 / total[HEAD : HEAD + 1, :])).astype(BF)

    def attend(t, half, first, stop, between):
        def body(i, carry):
            b = 3 - i
            made = attend_block(t, half, b)
            ot[t, half, 2 * b + 1] = made[:, TOK : 2 * TOK]
            ot[t, half, 2 * b] = made[:, 0:TOK]
            head_copy(t, half, 2 * b + 1, 2 * b + 2 - b // 3, b + 1).start()

            @pl.when(b > 0)
            def _():
                head_copy(t, half, 2 * b, 2 * b - 1, -b).start()

            for at, work in between.items():

                @pl.when(i == at)
                def _():
                    work()

            return carry

        lax.fori_loop(first, stop, body, 0)
        if stop == 4:
            mt[t, half, 0, 0:HEAD, :] = ot[t, half, 0]

    def part_copy(t, h):
        return to_partner(
            part_send.at[t, pl.ds(h * 64, 64), :], part_recv.at[t, pl.ds(h * 64, 64), :],
            part_ss.at[t, h], part_rs.at[t, h],
        )

    def heads_times_out(t, half):
        for p in range(1, 8):
            head_copy(t, half, p, p, 1).wait_recv()
        weights = wo[...].reshape(RING * HP, D)
        return tn(mt[t, half].reshape(RING * HP, TOK), weights)

    def project_pair(t):
        part_send[t] = heads_times_out(t, 1).astype(BF)
        for h in range(2):
            part_copy(t, h).start()

    def project_own(t):
        return heads_times_out(t, 0) + xs[t].astype(F32)

    def finish(t, h, own):
        rows = slice(h * 64, (h + 1) * 64)
        part_copy(t, h).wait_recv()
        x1[t, rows, :] = (own[rows] + part_recv[t, rows, :].astype(F32)).astype(BF)

    def down_copy(h):
        return pltpu.make_async_remote_copy(
            x1.at[0, pl.ds(h * 64, 64), :], down.at[pl.ds(h * 64, 64), :],
            down_ss.at[h], down_rs.at[h], device_id={"segment": above}, device_id_type=MESH,
        )

    def rise_copy():
        return pltpu.make_async_remote_copy(
            asc_out.at[0], operand.at[1, pl.ds(pl.multiple_of(y * TOK, 16), TOK), :],
            rise_ss.at[0], rise_rs.at[y], device_id={"segment": below, "ctx": z}, device_id_type=MESH,
        )

    def turn_copy():
        return pltpu.make_async_remote_copy(
            x1.at[0], operand.at[1, pl.ds(TOK, TOK), :],
            rise_ss.at[1], rise_rs.at[1], device_id={"ctx": partner}, device_id_type=MESH,
        )

    def mix_copy(t):
        return to_partner(asc_send.at[t], asc_recv.at[t], mix_ss.at[t], mix_rs.at[t])

    def ascend_first(t):
        asc_send[t] = jnp.dot(operand[t, TOK : 2 * TOK, :], wsk[...], preferred_element_type=F32).astype(BF)
        own_up[...] = jnp.dot(operand[t, 0:TOK, :], wsk[...], preferred_element_type=F32)

    def ascend_last(t):
        mix_copy(t).wait_recv()
        asc_out[t] = layer_norm(own_up[...] + asc_recv[t].astype(F32), gain_up).astype(BF)
        pltpu.make_async_copy(asc_out.at[t], asc_ref.at[t], store.at[1, t]).start()

    for j in range(4):
        rings[0].step(j)
    for copy in w_copies:
        copy.wait_recv()
    for g in range(3):
        project(0, g)
    rings[0].step(4)
    rings[0].step(5)
    loads[2].wait()
    out_ring.begin(0)
    project(0, 3)
    rings[0].step(6)
    out_ring.begin(1)
    project(0, 4)
    for g in range(5):
        for copy in pair_copies(0, g):
            copy.wait_recv()
    give_copies[0].start()
    pl.when(y == 0)(lambda: give_copies[1].start())
    attend(0, 1, 0, 4, {1: lambda: out_ring.step(0), 3: lambda: out_ring.step(1)})
    attend(0, 0, 0, 4, {1: lambda: out_ring.step(2), 3: lambda: out_ring.step(3)})
    loads[3].wait()
    out_ring.step(4)
    out_ring.step(5)
    skip_ring.begin(0)
    out_ring.step(6)
    skip_ring.begin(1)
    project_pair(0)
    own = project_own(0)
    skip_ring.step(0)
    skip_ring.step(1)
    for h in range(2):
        finish(0, h, own)
        down_copy(h).start()
    pltpu.make_async_copy(x1.at[0], desc_ref.at[0], store.at[0, 0]).start()

    last = s == SEGS - 1

    @pl.when(jnp.logical_and(last, y == 0))
    def _():
        operand[1, 0:TOK, :] = x1[0]

    @pl.when(jnp.logical_and(last, y == 1))
    def _():
        turn_copy().start()

    skip_ring.step(2)
    skip_ring.step(3)
    loads[6].wait()
    entering = queue[entry[0]]
    for h in range(2):
        rows = slice(h * 64, (h + 1) * 64)
        down_copy(h).wait_recv()
        xs[1, rows, :] = jnp.where(s == 0, entering[rows], down[rows, :])
        act[1, 0, rows, :] = layer_norm(xs[1, rows, :].astype(F32), gain_down).astype(BF)
    project(1, 0)
    skip_ring.step(4)
    rings[1].begin(0)
    skip_ring.step(5)
    rings[1].begin(1)
    skip_ring.step(6)

    give_copies[0].wait_recv()
    ascend_first(0)
    mix_copy(0).start()
    rings[1].step(0)
    rings[1].step(1)
    project(1, 1)
    rings[1].step(2)
    rings[1].step(3)
    project(1, 2)
    ascend_last(0)
    pl.when(s > 0)(lambda: rise_copy().start())

    @pl.when(y == 1)
    def _():
        give_copies[1].wait_recv()
        ascend_first(1)

    rings[1].step(4)
    rings[1].step(5)
    project(1, 3)
    rings[1].step(6)
    project(1, 4)

    @pl.when(jnp.logical_and(y == 0, s < SEGS - 1))
    def _():
        pltpu.make_async_remote_copy(
            asc_out.at[0], operand.at[1, pl.ds(0, TOK), :], rise_ss.at[0], rise_rs.at[0],
            device_id={"segment": below, "ctx": z}, device_id_type=MESH,
        ).wait_recv()

    @pl.when(y == 0)
    def _():
        turn_copy().wait_recv()
        ascend_first(1)

    for g in range(5):
        for copy in pair_copies(1, g):
            copy.wait_recv()
    mix_copy(1).start()
    attend(1, 1, 0, 4, {})
    attend(1, 0, 0, 2, {})
    project_pair(1)
    attend(1, 0, 2, 4, {})
    ascend_last(1)
    own = project_own(1)
    for h in range(2):
        finish(1, h, own)
    pltpu.make_async_copy(x1.at[1], desc_ref.at[1], store.at[0, 1]).start()

    for ring in (*rings, out_ring, skip_ring):
        ring.drain()
    for copy in w_copies:
        copy.wait_send()
    give_copies[0].wait_send()
    pl.when(y == 0)(lambda: give_copies[1].wait_send())
    for t in range(2):
        for g in range(5):
            for copy in pair_copies(t, g):
                copy.wait_send()
        mix_copy(t).wait_send()
        for half in range(2):
            for p in range(1, 8):
                head_copy(t, half, p, p, 1).wait_send()
        for h in range(2):
            part_copy(t, h).wait_send()
    for h in range(2):
        down_copy(h).wait_send()
    pl.when(s > 0)(lambda: rise_copy().wait_send())
    pl.when(jnp.logical_and(last, y == 1))(lambda: turn_copy().wait_send())
    for t in range(2):
        pltpu.make_async_copy(x1.at[t], desc_ref.at[t], store.at[0, t]).wait()
        pltpu.make_async_copy(asc_out.at[t], asc_ref.at[t], store.at[1, t]).wait()


def hand_on(desc_in, asc_in, desc_ref, asc_ref, held, read, write):
    ends = ((desc_in, desc_ref), (asc_in, asc_ref))
    pieces = [(a, t, h) for t in range(2) for a in range(2) for h in range(2)]

    def fetch(a, t, h):
        rows = pl.ds(h * 64, 64)
        return pltpu.make_async_copy(ends[a][0].at[t, rows, :], held.at[a, t, rows, :], read.at[a, t, h])

    def put(a, t, h):
        rows = pl.ds(h * 64, 64)
        return pltpu.make_async_copy(held.at[a, t, rows, :], ends[a][1].at[t, rows, :], write.at[a, t, h])

    for piece in pieces:
        fetch(*piece).start()
    for piece in pieces:
        fetch(*piece).wait()
        put(*piece).start()
    for piece in pieces:
        put(*piece).wait()


def on_device(
    carried_down, carried_up, skip_bank, queue, next_entry, skip_slot, w_qkv, w_out, w_skip, gains
):
    hbm = pl.BlockSpec(memory_space=pl.ANY)
    smem = pl.BlockSpec(memory_space=pltpu.SMEM)
    vmem = pl.BlockSpec(memory_space=pltpu.VMEM)
    dma = pltpu.SemaphoreType.DMA
    V = pltpu.VMEM
    scratch = [
        V((3, TOK, D), BF),
        V((TOK, D), BF),
        V((3, TOK, D), BF),
        V((8, TOK, D), BF),
        V((3, HEAD, D), BF),
        V((2, RING, TOK, D), BF),
        V((4 * HP, D), BF),
        V((256, D), BF),
        V((2, 2, 128, 1024), BF),
        V((2, 2048, 128), BF),
        V((2, HP, 2048), BF),
        V((2, HEAD, 1024), BF),
        V((2, 1024, 128), BF),
        V((2, HEAD, 1024), BF),
        V((8, 256, 256), F32),
        V((2, 2, RING, HEAD, TOK), BF),
        V((2, 2, RING, HP, TOK), BF),
        V((RING, HP, D), BF),
        V((D, D), BF),
        V((2, TOK, D), BF),
        V((2, TOK, D), BF),
        V((2, TOK, D), BF),
        V((2, 2 * TOK, D), BF),
        V((2, TOK, D), BF),
        V((2, TOK, D), BF),
        V((2, TOK, D), BF),
        V((2, TOK, D), BF),
        V((TOK, D), F32),
        dma((7,)), dma((2, 2)),
        dma((2, 2, 7)), dma((2, 2, 7)), dma((2, 7)), dma((2, 7)), dma((2, 7)), dma((2, 7)),
        dma((2, 5, 3)), dma((2, 5, 3)), dma((3,)), dma((3,)), dma((2, 2, 8)), dma((2, 2, 8)),
        dma((2, 2)), dma((2, 2)), dma((2,)), dma((2,)), dma((2,)), dma((2,)),
        dma((2,)), dma((2,)), dma((2,)), dma((2,)),
    ]
    desc, asc = pl.pallas_call(
        kernel,
        out_shape=(
            jax.ShapeDtypeStruct((2, TOK, D), BF),
            jax.ShapeDtypeStruct((2, TOK, D), BF),
        ),
        in_specs=[hbm, hbm, hbm, hbm, smem, smem, hbm, hbm, hbm, vmem],
        out_specs=(hbm, hbm),
        scratch_shapes=scratch,
        compiler_params=pltpu.CompilerParams(
            collective_id=0, has_side_effects=True, vmem_limit_bytes=60 * 1024 * 1024
        ),
    )(
        carried_down[0], carried_up[0], skip_bank[0], queue, next_entry, skip_slot.T,
        w_qkv[0], w_out[0], w_skip[0], gains[0],
    )
    desc, asc = pl.pallas_call(
        hand_on,
        out_shape=(
            jax.ShapeDtypeStruct((2, TOK, D), BF),
            jax.ShapeDtypeStruct((2, TOK, D), BF),
        ),
        in_specs=[hbm, hbm],
        out_specs=(hbm, hbm),
        scratch_shapes=[V((2, 2, TOK, D), BF), dma((2, 2, 2)), dma((2, 2, 2))],
        compiler_params=pltpu.CompilerParams(vmem_limit_bytes=60 * 1024 * 1024),
    )(desc, asc)
    return desc[:, None], asc[:, None]


def solution(mesh):
    in_specs = (
        P("segment", "ctx", None),
        P("segment", "ctx", None),
        P("segment", None, "ctx", None),
        P(None, "ctx", None),
        P(),
        P(None, "segment"),
        P("segment", None, "ctx", None),
        P("segment", "ctx", None),
        P("segment", "ctx", None),
        P("segment", None, None),
    )
    out_specs = (P(None, "segment", "ctx", None), P(None, "segment", "ctx", None))
    return jax.shard_map(
        on_device, mesh=mesh, in_specs=in_specs, out_specs=out_specs, check_vma=False
    )
```

```python
import jax
import jax.numpy as jnp
from jax import lax
from jax.experimental import pallas as pl
from jax.experimental.pallas import tpu as pltpu
from jax.sharding import PartitionSpec as P

HEAD = 88
HP = 96
D = 1408
TOK = 128
RING = 8
SEGS = 16
ROWS = 176
SCALE = HEAD**-0.5
LOG2E = 1.4426950408889634
MESH = pl.DeviceIdType.MESH
BF = jnp.bfloat16
F32 = jnp.float32
GROUPS = ((0, 1), (1, 3), (3, 5), (5, 7), (7, 8))
EARLY = tuple((ring + start, size) for ring in (0, 1024) for start, size in ((0, 256), (256, 256), (512, 256), (768, 128)))


def slot_of(delta):
    if delta == 0:
        return 0
    if abs(delta) == 4:
        return 7
    return 2 * delta - 1 if delta > 0 else -2 * delta


def nt(a, b):
    return lax.dot_general(a, b, (((1,), (1,)), ((), ())), preferred_element_type=F32)


def tn(a, b):
    return lax.dot_general(a, b, (((0,), (0,)), ((), ())), preferred_element_type=F32)


def layer_norm(x, gain):
    center = x - jnp.mean(x, axis=-1, keepdims=True)
    spread = jnp.mean(center * center, axis=-1, keepdims=True)
    return center * lax.rsqrt(spread + 1e-06) * gain


class Ring:
    def __init__(self, peers, send, recv, src, dst):
        self.peers, self.send, self.recv, self.src, self.dst = peers, send, recv, src, dst

    def copy(self, way, j):
        hops, half = j // 2, (way if j == 6 else j % 2)
        return pltpu.make_async_remote_copy(
            self.src(way, hops, half),
            self.dst(way, hops, half),
            self.send.at[way, j],
            self.recv.at[way, j],
            device_id={"ctx": self.peers[way]},
            device_id_type=MESH,
        )

    def start(self, way, j):
        self.copy(way, j).start()

    def arrive(self, way, j):
        hops, half = j // 2, (way if j == 6 else j % 2)
        here = self.src(way, hops + 1, half)
        pltpu.make_async_remote_copy(
            here,
            here,
            self.send.at[way, j],
            self.recv.at[way, j],
            device_id={"ctx": self.peers[way]},
            device_id_type=MESH,
        ).wait_recv()

    def begin(self, half):
        self.start(0, half)
        self.start(1, half)

    def step(self, j):
        for way in (0, 1):
            self.arrive(way, j)
            if j < 4:
                self.start(way, j + 2)
            elif j == 4 + way:
                self.start(way, 6)

    def drain(self):
        for way in (0, 1):
            for j in range(7):
                self.copy(way, j).wait_send()


def slot_ring(peers, send, recv, view):
    def src(way, hops, half):
        return view(slot_of(-hops if way == 0 else hops), half)

    def dst(way, hops, half):
        return view(slot_of(-hops - 1 if way == 0 else hops + 1), half)

    return Ring(peers, send, recv, src, dst)


def row_ring(peers, send, recv, z, buf):
    def src(way, hops, half):
        origin = lax.rem(z + (8 - hops if way == 0 else hops), 8)
        start = pl.multiple_of(origin * ROWS + half * 96, 16)
        return buf.at[pl.ds(start, 80 if half else 96), :]

    return Ring(peers, send, recv, src, src)


def kernel(
    x_in, up_in, bank_in, queue_in, entry, slots, qkv_in, out_in, skip_in, gains,
    desc_ref, asc_ref,
    xs, down, bank, queue, stage_qkv, act, wqv, wk, qt, kk, vt, qs, ks, vs, scores, ot, mt,
    wo, wsk, part_send, part_recv, x1, operand, give, asc_send, asc_recv, asc_out, own_up, early_peak, early_total,
    load, store, act_send, act_recv, wo_send, wo_recv, wsk_send, wsk_recv,
    pair_send, pair_recv, w_send, w_recv, head_send, head_recv,
    swap_send, swap_recv, part_ss, part_rs, down_ss, down_rs, give_ss, give_rs, rise_ss, rise_rs, mix_ss, mix_rs,
):
    s = lax.axis_index("segment")
    c = lax.axis_index("ctx")
    y, z = c // 8, c % 8
    partner = (1 - y) * 8 + z
    above, below = (s + 1) % SEGS, (s + SEGS - 1) % SEGS

    def ring_peer(delta):
        return y * 8 + (z + delta + 8) % 8

    peers = (ring_peer(1), ring_peer(-1))

    loads = [
        pltpu.make_async_copy(x_in, xs.at[0], load.at[0]),
        pltpu.make_async_copy(qkv_in, stage_qkv, load.at[1]),
        pltpu.make_async_copy(out_in, wo.at[0, pl.ds(0, HEAD), :], load.at[2]),
        pltpu.make_async_copy(skip_in, wsk.at[pl.ds(pl.multiple_of(z * ROWS, 16), ROWS), :], load.at[3]),
        pltpu.make_async_copy(up_in, xs.at[2], load.at[4]),
        pltpu.make_async_copy(bank_in, bank, load.at[5]),
        pltpu.make_async_copy(queue_in, queue, load.at[6]),
    ]
    for copy in loads:
        copy.start()

    barrier = pltpu.get_barrier_semaphore()
    diagonal = {"segment": (s + SEGS + 1 - 2 * y) % SEGS, "ctx": partner}
    greet = [{"ctx": ring_peer(d)} for d in (1, -1)]
    greet += [{"ctx": partner}, {"segment": above}, {"segment": below}, diagonal]
    for peer in greet:
        pl.semaphore_signal(barrier, inc=1, device_id=peer, device_id_type=MESH)

    pad = HP - HEAD
    wo[:, HEAD:HP, :] = jnp.zeros((2 * RING, pad, D), BF)
    for block in range(4):
        wqv[block * HP + HEAD : (block + 1) * HP, :] = jnp.zeros((pad, D), BF)
    for block in range(2):
        wk[block * 128 + HEAD : (block + 1) * 128, :] = jnp.zeros((128 - HEAD, D), BF)
    qt[:, :, HEAD:128, :] = jnp.zeros((2, 2, 128 - HEAD, 1024), BF)
    mt[:, :, :, HEAD:HP, :] = jnp.zeros((2, 2, RING, pad, TOK), BF)
    ones = (lax.broadcasted_iota(jnp.int32, (pad, 2048), 0) == 0).astype(F32).astype(BF)
    for t in range(2):
        vt[t, HEAD:HP, :] = ones

    gain_down, gain_up = gains[0:1, :], gains[1:2, :]
    loads[0].wait()
    act[0, 0] = layer_norm(xs[0].astype(F32), gain_down).astype(BF)
    loads[1].wait()
    wqv[0:HEAD, :] = stage_qkv[0]
    wqv[HP : HP + HEAD, :] = stage_qkv[2]
    wk[0:HEAD, :] = stage_qkv[1]
    loads[4].wait()
    loads[5].wait()
    skip_first = bank[slots[0, 0]]
    skip_second = bank[slots[0, 1]]
    rising = xs[2]
    operand[0, 0:TOK, :] = jnp.where(y == 0, rising, skip_first)
    give[0] = jnp.where(y == 0, skip_first, rising)
    give[1] = skip_second

    @pl.when(y == 1)
    def _():
        operand[1, 0:TOK, :] = skip_second

    def act_ring(t):
        return slot_ring(
            peers, act_send.at[t], act_recv.at[t],
            lambda p, half: act.at[t, p, pl.ds(half * 64, 64), :],
        )

    rings = [act_ring(0), act_ring(1)]
    out_ring = slot_ring(peers, wo_send, wo_recv, lambda p, half: wo.at[p, pl.ds(half * 48, 40 if half else 48), :])
    skip_ring = row_ring(peers, wsk_send, wsk_recv, z, wsk)

    def to_partner(src, dst, send, recv):
        return pltpu.make_async_remote_copy(
            src, dst, send, recv, device_id={"ctx": partner}, device_id_type=MESH
        )

    w_copies = [
        to_partner(wqv.at[pl.ds(0, HEAD), :], wqv.at[pl.ds(2 * HP, HEAD), :], w_send.at[0], w_recv.at[0]),
        to_partner(wqv.at[pl.ds(HP, HEAD), :], wqv.at[pl.ds(3 * HP, HEAD), :], w_send.at[1], w_recv.at[1]),
        to_partner(wk.at[pl.ds(0, HEAD), :], wk.at[pl.ds(128, HEAD), :], w_send.at[2], w_recv.at[2]),
    ]
    give_copies = [
        to_partner(give.at[t], operand.at[t, pl.ds(TOK, TOK), :], give_ss.at[t], give_rs.at[t])
        for t in range(2)
    ]

    pl.semaphore_wait(barrier, len(greet))
    rings[0].begin(0)
    rings[0].begin(1)
    for copy in w_copies:
        copy.start()

    def pair_copies(t, g):
        lo, hi = GROUPS[g]
        n = (hi - lo) * TOK
        return [
            to_partner(
                qs.at[t, :, pl.ds(lo * TOK, n)],
                qt.at[t, 1, pl.ds(0, HEAD), pl.ds(lo * TOK, n)],
                pair_send.at[t, g, 0], pair_recv.at[t, g, 0],
            ),
            to_partner(
                ks.at[t, pl.ds(lo * TOK, n), :],
                kk.at[t, pl.ds(1024 + lo * TOK, n), :],
                pair_send.at[t, g, 1], pair_recv.at[t, g, 1],
            ),
            to_partner(
                vs.at[t, :, pl.ds(lo * TOK, n)],
                vt.at[t, pl.ds(0, HEAD), pl.ds(1024 + lo * TOK, n)],
                pair_send.at[t, g, 2], pair_recv.at[t, g, 2],
            ),
        ]

    def project(t, g):
        lo, hi = GROUPS[g]
        n = (hi - lo) * TOK
        tokens = act[t, lo:hi].reshape(n, D)
        made = nt(wqv[...], tokens)
        keys = nt(tokens, wk[...]).astype(BF)
        own_q = (made[0:HEAD] * (SCALE * LOG2E)).astype(BF)
        pair_q = (made[2 * HP : 2 * HP + HEAD] * (SCALE * LOG2E)).astype(BF)
        made = made.astype(BF)
        qt[t, 0, 0:HEAD, lo * TOK : hi * TOK] = own_q
        vt[t, 0:HEAD, lo * TOK : hi * TOK] = made[HP : HP + HEAD]
        qs[t, :, lo * TOK : hi * TOK] = pair_q
        vs[t, :, lo * TOK : hi * TOK] = made[3 * HP : 3 * HP + HEAD]
        kk[t, lo * TOK : hi * TOK, :] = keys[:, 0:128]
        ks[t, lo * TOK : hi * TOK, :] = keys[:, 128:256]
        for copy in pair_copies(t, g):
            copy.start()

    def head_copy(t, half, p, mirror, delta):
        ring = 1 - y if t == 1 and half == 1 else y
        return pltpu.make_async_remote_copy(
            ot.at[t, half, p], mt.at[t, half, mirror, pl.ds(0, HEAD), :],
            head_send.at[t, half, p], head_recv.at[t, half, mirror],
            device_id={"ctx": ring * 8 + (z + delta + 8) % 8}, device_id_type=MESH,
        )

    def swap_copy(p):
        return to_partner(
            wo.at[p, pl.ds(0, HEAD), :], wo.at[RING + p, pl.ds(0, HEAD), :], swap_send.at[p], swap_recv.at[p]
        )

    def attend_block(t, half, b):
        queries = qt[t, half, :, pl.ds(pl.multiple_of(b * 256, 256), 256)]
        peak = None
        for kb in range(8):
            made = jnp.dot(kk[t, kb * 256 : (kb + 1) * 256, :], queries, preferred_element_type=F32)
            scores[kb] = made
            top = jnp.max(made.reshape(32, 8, 256), axis=0)
            peak = top if peak is None else jnp.maximum(peak, top)
        peak = jnp.max(peak, axis=0, keepdims=True)
        total = jnp.zeros((HP, 256), F32)
        for kb in range(8):
            powers = jnp.exp2(scores[kb] - peak).astype(BF)
            total += jnp.dot(vt[t, :, kb * 256 : (kb + 1) * 256], powers, preferred_element_type=F32)
        return (total[0:HEAD] * (1.0 / total[HEAD : HEAD + 1, :])).astype(BF)

    def attend_early(b):
        queries = qt[1, 1, :, pl.ds(pl.multiple_of(b * 256, 256), 256)]
        peak = None
        for kb, (start, size) in enumerate(EARLY):
            made = jnp.dot(kk[1, start : start + size, :], queries, preferred_element_type=F32)
            scores[kb, 0:size, :] = made
            top = jnp.max(made.reshape(size // 8, 8, 256), axis=0)
            peak = top if peak is None else jnp.maximum(peak, top)
        peak = jnp.max(peak, axis=0, keepdims=True)
        total = jnp.zeros((HP, 256), F32)
        for kb, (start, size) in enumerate(EARLY):
            powers = jnp.exp2(scores[kb, 0:size, :] - peak).astype(BF)
            total += jnp.dot(vt[1, :, start : start + size], powers, preferred_element_type=F32)
        early_peak[b] = jnp.broadcast_to(peak, (8, 256))
        early_total[b] = total

    def attend_late(b):
        queries = qt[1, 1, :, pl.ds(pl.multiple_of(b * 256, 256), 256)]
        keys = jnp.concatenate([kk[1, 896:1024, :], kk[1, 1920:2048, :]], axis=0)
        values = jnp.concatenate([vt[1, :, 896:1024], vt[1, :, 1920:2048]], axis=1)
        made = jnp.dot(keys, queries, preferred_element_type=F32)
        before = early_peak[b][0:1, :]
        peak = jnp.maximum(before, jnp.max(jnp.max(made.reshape(32, 8, 256), axis=0), axis=0, keepdims=True))
        powers = jnp.exp2(made - peak).astype(BF)
        total = early_total[b] * jnp.exp2(before - peak)
        total += jnp.dot(values, powers, preferred_element_type=F32)
        return (total[0:HEAD] * (1.0 / total[HEAD : HEAD + 1, :])).astype(BF)

    def pass_on(t, half, b, made):
        ot[t, half, 2 * b + 1] = made[:, TOK : 2 * TOK]
        ot[t, half, 2 * b] = made[:, 0:TOK]
        head_copy(t, half, 2 * b + 1, 2 * b + 2 - b // 3, b + 1).start()

        @pl.when(b > 0)
        def _():
            head_copy(t, half, 2 * b, 2 * b - 1, -b).start()

    def attend(t, half, first, stop, between, block=None):
        def body(i, carry):
            b = 3 - i
            pass_on(t, half, b, attend_block(t, half, b) if block is None else block(b))
            for at, work in between.items():

                @pl.when(i == at)
                def _():
                    work()

            return carry

        lax.fori_loop(first, stop, body, 0)
        if stop == 4 and t == 1 and half == 1:
            head_copy(t, half, 0, 0, 0).start()
        elif stop == 4:
            mt[t, half, 0, 0:HEAD, :] = ot[t, half, 0]

    def part_copy(h):
        return to_partner(
            part_send.at[pl.ds(h * 64, 64), :], part_recv.at[pl.ds(h * 64, 64), :],
            part_ss.at[h], part_rs.at[h],
        )

    def heads_times_out(t, half, slots):
        for p in range(1 if t == 0 or half == 0 else 0, 8):
            head_copy(t, half, p, p, 1).wait_recv()
        weights = wo[slots : slots + RING].reshape(RING * HP, D)
        return tn(mt[t, half].reshape(RING * HP, TOK), weights)

    def project_pair():
        part_send[...] = heads_times_out(0, 1, 0).astype(BF)
        for h in range(2):
            part_copy(h).start()

    def finish(h, own):
        rows = slice(h * 64, (h + 1) * 64)
        part_copy(h).wait_recv()
        x1[0, rows, :] = (own[rows] + part_recv[rows, :].astype(F32)).astype(BF)

    def down_copy(h):
        return pltpu.make_async_remote_copy(
            x1.at[0, pl.ds(h * 64, 64), :], down.at[pl.ds(h * 64, 64), :],
            down_ss.at[h], down_rs.at[h], device_id={"segment": above}, device_id_type=MESH,
        )

    def rise_copy():
        return pltpu.make_async_remote_copy(
            asc_out.at[0], operand.at[1, pl.ds(pl.multiple_of(y * TOK, 16), TOK), :],
            rise_ss.at[0], rise_rs.at[y], device_id={"segment": below, "ctx": z}, device_id_type=MESH,
        )

    def turn_copy():
        return pltpu.make_async_remote_copy(
            x1.at[0], operand.at[1, pl.ds(TOK, TOK), :],
            rise_ss.at[1], rise_rs.at[1], device_id={"ctx": partner}, device_id_type=MESH,
        )

    def mix_copy(t):
        return to_partner(asc_send.at[t], asc_recv.at[t], mix_ss.at[t], mix_rs.at[t])

    def ascend_first(t):
        asc_send[t] = jnp.dot(operand[t, TOK : 2 * TOK, :], wsk[...], preferred_element_type=F32).astype(BF)
        own_up[...] = jnp.dot(operand[t, 0:TOK, :], wsk[...], preferred_element_type=F32)

    def ascend_last(t):
        mix_copy(t).wait_recv()
        asc_out[t] = layer_norm(own_up[...] + asc_recv[t].astype(F32), gain_up).astype(BF)
        pltpu.make_async_copy(asc_out.at[t], asc_ref.at[t], store.at[1, t]).start()

    for j in range(4):
        rings[0].step(j)
    for copy in w_copies:
        copy.wait_recv()
    for g in range(3):
        project(0, g)
    rings[0].step(4)
    rings[0].step(5)
    loads[2].wait()
    out_ring.begin(0)
    project(0, 3)
    rings[0].step(6)
    out_ring.begin(1)
    project(0, 4)
    for g in range(5):
        for copy in pair_copies(0, g):
            copy.wait_recv()
    swap_copy(0).start()

    def out_step(j):
        def work():
            out_ring.step(j)
            if j % 2:
                swap_copy(j).start()
                swap_copy(j + 1).start()

        return work

    attend(0, 1, 0, 4, {1: out_step(0), 3: out_step(1)})
    attend(0, 0, 0, 4, {1: out_step(2), 3: out_step(3)})
    loads[3].wait()
    out_ring.step(4)
    out_ring.step(5)
    skip_ring.begin(0)
    out_ring.step(6)
    skip_ring.begin(1)
    project_pair()
    own = heads_times_out(0, 0, 0) + xs[0].astype(F32)
    skip_ring.step(0)
    skip_ring.step(1)
    for h in range(2):
        finish(h, own)
        down_copy(h).start()
    for p in range(5, 8):
        swap_copy(p).start()
    give_copies[0].start()
    pl.when(y == 0)(lambda: give_copies[1].start())
    pltpu.make_async_copy(x1.at[0], desc_ref.at[0], store.at[0, 0]).start()

    last = s == SEGS - 1

    @pl.when(jnp.logical_and(last, y == 0))
    def _():
        operand[1, 0:TOK, :] = x1[0]

    @pl.when(jnp.logical_and(last, y == 1))
    def _():
        turn_copy().start()

    skip_ring.step(2)
    skip_ring.step(3)
    loads[6].wait()
    entering = queue[entry[0]]
    for h in range(2):
        rows = slice(h * 64, (h + 1) * 64)
        down_copy(h).wait_recv()
        xs[1, rows, :] = jnp.where(s == 0, entering[rows], down[rows, :])
        act[1, 0, rows, :] = layer_norm(xs[1, rows, :].astype(F32), gain_down).astype(BF)
    project(1, 0)
    skip_ring.step(4)
    rings[1].begin(0)
    skip_ring.step(5)
    rings[1].begin(1)
    skip_ring.step(6)

    give_copies[0].wait_recv()
    ascend_first(0)
    mix_copy(0).start()
    rings[1].step(0)
    rings[1].step(1)
    project(1, 1)
    rings[1].step(2)
    rings[1].step(3)
    project(1, 2)
    ascend_last(0)
    pl.when(s > 0)(lambda: rise_copy().start())

    @pl.when(y == 1)
    def _():
        give_copies[1].wait_recv()
        ascend_first(1)

    rings[1].step(4)
    rings[1].step(5)
    project(1, 3)
    rings[1].step(6)
    project(1, 4)

    @pl.when(jnp.logical_and(y == 0, s < SEGS - 1))
    def _():
        pltpu.make_async_remote_copy(
            asc_out.at[0], operand.at[1, pl.ds(0, TOK), :], rise_ss.at[0], rise_rs.at[0],
            device_id={"segment": below, "ctx": z}, device_id_type=MESH,
        ).wait_recv()

    @pl.when(y == 0)
    def _():
        turn_copy().wait_recv()
        ascend_first(1)

    for g in range(4):
        for copy in pair_copies(1, g):
            copy.wait_recv()

    def early(i, carry):
        attend_early(2 - i)
        return carry

    mix_copy(1).start()
    lax.fori_loop(0, 3, early, 0)
    for copy in pair_copies(1, 4):
        copy.wait_recv()
    attend(1, 1, 0, 1, {})
    attend(1, 1, 1, 4, {}, attend_late)
    attend(1, 0, 0, 4, {})
    for p in range(8):
        swap_copy(p).wait_recv()
    own = heads_times_out(1, 1, RING) + xs[1].astype(F32)
    x1[1] = (own + heads_times_out(1, 0, 0)).astype(BF)
    pltpu.make_async_copy(x1.at[1], desc_ref.at[1], store.at[0, 1]).start()
    ascend_last(1)

    for ring in (*rings, out_ring, skip_ring):
        ring.drain()
    for copy in w_copies:
        copy.wait_send()
    give_copies[0].wait_send()
    pl.when(y == 0)(lambda: give_copies[1].wait_send())
    for t in range(2):
        for g in range(5):
            for copy in pair_copies(t, g):
                copy.wait_send()
        mix_copy(t).wait_send()
        for half in range(2):
            for p in range(1 if t == 0 or half == 0 else 0, 8):
                head_copy(t, half, p, p, 1).wait_send()
    for p in range(8):
        swap_copy(p).wait_send()
    for h in range(2):
        part_copy(h).wait_send()
        down_copy(h).wait_send()
    pl.when(s > 0)(lambda: rise_copy().wait_send())
    pl.when(jnp.logical_and(last, y == 1))(lambda: turn_copy().wait_send())
    for t in range(2):
        pltpu.make_async_copy(x1.at[t], desc_ref.at[t], store.at[0, t]).wait()
        pltpu.make_async_copy(asc_out.at[t], asc_ref.at[t], store.at[1, t]).wait()


def hand_on(desc_in, asc_in, desc_ref, asc_ref, held, read, write):
    ends = ((desc_in, desc_ref), (asc_in, asc_ref))
    pieces = [(a, t, h) for t in range(2) for a in range(2) for h in range(2)]

    def fetch(a, t, h):
        rows = pl.ds(h * 64, 64)
        return pltpu.make_async_copy(ends[a][0].at[t, rows, :], held.at[a, t, rows, :], read.at[a, t, h])

    def put(a, t, h):
        rows = pl.ds(h * 64, 64)
        return pltpu.make_async_copy(held.at[a, t, rows, :], ends[a][1].at[t, rows, :], write.at[a, t, h])

    for piece in pieces:
        fetch(*piece).start()
    for piece in pieces:
        fetch(*piece).wait()
        put(*piece).start()
    for piece in pieces:
        put(*piece).wait()


def on_device(
    carried_down, carried_up, skip_bank, queue, next_entry, skip_slot, w_qkv, w_out, w_skip, gains
):
    hbm = pl.BlockSpec(memory_space=pl.ANY)
    smem = pl.BlockSpec(memory_space=pltpu.SMEM)
    vmem = pl.BlockSpec(memory_space=pltpu.VMEM)
    dma = pltpu.SemaphoreType.DMA
    V = pltpu.VMEM
    scratch = [
        V((3, TOK, D), BF),
        V((TOK, D), BF),
        V((3, TOK, D), BF),
        V((8, TOK, D), BF),
        V((3, HEAD, D), BF),
        V((2, RING, TOK, D), BF),
        V((4 * HP, D), BF),
        V((256, D), BF),
        V((2, 2, 128, 1024), BF),
        V((2, 2048, 128), BF),
        V((2, HP, 2048), BF),
        V((2, HEAD, 1024), BF),
        V((2, 1024, 128), BF),
        V((2, HEAD, 1024), BF),
        V((8, 256, 256), F32),
        V((2, 2, RING, HEAD, TOK), BF),
        V((2, 2, RING, HP, TOK), BF),
        V((2 * RING, HP, D), BF),
        V((D, D), BF),
        V((TOK, D), BF),
        V((TOK, D), BF),
        V((2, TOK, D), BF),
        V((2, 2 * TOK, D), BF),
        V((2, TOK, D), BF),
        V((2, TOK, D), BF),
        V((2, TOK, D), BF),
        V((2, TOK, D), BF),
        V((TOK, D), F32),
        V((3, 8, 256), F32),
        V((3, HP, 256), F32),
        dma((7,)), dma((2, 2)),
        dma((2, 2, 7)), dma((2, 2, 7)), dma((2, 7)), dma((2, 7)), dma((2, 7)), dma((2, 7)),
        dma((2, 5, 3)), dma((2, 5, 3)), dma((3,)), dma((3,)), dma((2, 2, 8)), dma((2, 2, 8)),
        dma((8,)), dma((8,)), dma((2,)), dma((2,)), dma((2,)), dma((2,)), dma((2,)), dma((2,)),
        dma((2,)), dma((2,)), dma((2,)), dma((2,)),
    ]
    desc, asc = pl.pallas_call(
        kernel,
        out_shape=(
            jax.ShapeDtypeStruct((2, TOK, D), BF),
            jax.ShapeDtypeStruct((2, TOK, D), BF),
        ),
        in_specs=[hbm, hbm, hbm, hbm, smem, smem, hbm, hbm, hbm, vmem],
        out_specs=(hbm, hbm),
        scratch_shapes=scratch,
        compiler_params=pltpu.CompilerParams(
            collective_id=0, has_side_effects=True, vmem_limit_bytes=60 * 1024 * 1024
        ),
    )(
        carried_down[0], carried_up[0], skip_bank[0], queue, next_entry, skip_slot.T,
        w_qkv[0], w_out[0], w_skip[0], gains[0],
    )
    desc, asc = pl.pallas_call(
        hand_on,
        out_shape=(
            jax.ShapeDtypeStruct((2, TOK, D), BF),
            jax.ShapeDtypeStruct((2, TOK, D), BF),
        ),
        in_specs=[hbm, hbm],
        out_specs=(hbm, hbm),
        scratch_shapes=[V((2, 2, TOK, D), BF), dma((2, 2, 2)), dma((2, 2, 2))],
        compiler_params=pltpu.CompilerParams(vmem_limit_bytes=60 * 1024 * 1024),
    )(desc, asc)
    return desc[:, None], asc[:, None]


def solution(mesh):
    in_specs = (
        P("segment", "ctx", None),
        P("segment", "ctx", None),
        P("segment", None, "ctx", None),
        P(None, "ctx", None),
        P(),
        P(None, "segment"),
        P("segment", None, "ctx", None),
        P("segment", "ctx", None),
        P("segment", "ctx", None),
        P("segment", None, None),
    )
    out_specs = (P(None, "segment", "ctx", None), P(None, "segment", "ctx", None))
    return jax.shard_map(
        on_device, mesh=mesh, in_specs=in_specs, out_specs=out_specs, check_vma=False
    )
```

```python
import jax
import jax.numpy as jnp
from jax import lax
from jax.experimental import pallas as pl
from jax.experimental.pallas import tpu as pltpu
from jax.sharding import PartitionSpec as P

HEAD = 88
HP = 96
D = 1408
TOK = 128
RING = 8
SEGS = 16
ROWS = 176
SCALE = HEAD**-0.5
LOG2E = 1.4426950408889634
MESH = pl.DeviceIdType.MESH
BF = jnp.bfloat16
F32 = jnp.float32
GROUPS = ((0, 1), (1, 3), (3, 5), (5, 7), (7, 8))
EARLY = tuple((ring + start, size) for ring in (0, 1024) for start, size in ((0, 256), (256, 256), (512, 256), (768, 128)))


def slot_of(delta):
    if delta == 0:
        return 0
    if abs(delta) == 4:
        return 7
    return 2 * delta - 1 if delta > 0 else -2 * delta


def nt(a, b):
    return lax.dot_general(a, b, (((1,), (1,)), ((), ())), preferred_element_type=F32)


def tn(a, b):
    return lax.dot_general(a, b, (((0,), (0,)), ((), ())), preferred_element_type=F32)


def layer_norm(x, gain):
    center = x - jnp.mean(x, axis=-1, keepdims=True)
    spread = jnp.mean(center * center, axis=-1, keepdims=True)
    return center * lax.rsqrt(spread + 1e-06) * gain


class Ring:
    def __init__(self, peers, send, recv, src, dst):
        self.peers, self.send, self.recv, self.src, self.dst = peers, send, recv, src, dst

    def copy(self, way, j):
        hops, half = j // 2, (way if j == 6 else j % 2)
        return pltpu.make_async_remote_copy(
            self.src(way, hops, half),
            self.dst(way, hops, half),
            self.send.at[way, j],
            self.recv.at[way, j],
            device_id={"ctx": self.peers[way]},
            device_id_type=MESH,
        )

    def start(self, way, j):
        self.copy(way, j).start()

    def arrive(self, way, j):
        hops, half = j // 2, (way if j == 6 else j % 2)
        here = self.src(way, hops + 1, half)
        pltpu.make_async_remote_copy(
            here,
            here,
            self.send.at[way, j],
            self.recv.at[way, j],
            device_id={"ctx": self.peers[way]},
            device_id_type=MESH,
        ).wait_recv()

    def begin(self, half):
        self.start(0, half)
        self.start(1, half)

    def step(self, j):
        for way in (0, 1):
            self.arrive(way, j)
            if j < 4:
                self.start(way, j + 2)
            elif j == 4 + way:
                self.start(way, 6)

    def drain(self):
        for way in (0, 1):
            for j in range(7):
                self.copy(way, j).wait_send()


def slot_ring(peers, send, recv, view):
    def src(way, hops, half):
        return view(slot_of(-hops if way == 0 else hops), half)

    def dst(way, hops, half):
        return view(slot_of(-hops - 1 if way == 0 else hops + 1), half)

    return Ring(peers, send, recv, src, dst)


def row_ring(peers, send, recv, z, buf):
    def src(way, hops, half):
        origin = lax.rem(z + (8 - hops if way == 0 else hops), 8)
        start = pl.multiple_of(origin * ROWS + half * 96, 16)
        return buf.at[pl.ds(start, 80 if half else 96), :]

    return Ring(peers, send, recv, src, src)


def kernel(
    x_in, up_in, bank_in, queue_in, entry, slots, qkv_in, out_in, skip_in, gains,
    desc_ref, asc_ref,
    xs, down, bank, queue, stage_qkv, act, wqv, wk, qt, kk, vt, qs, ks, kt, vs, scores, ot, mt,
    wo, wsk, part_send, part_recv, x1, operand, give, asc_send, asc_recv, asc_out, own_up, early_peak, early_total,
    load, store, act_send, act_recv, wo_send, wo_recv, wsk_send, wsk_recv,
    pair_send, pair_recv, w_send, w_recv, head_send, head_recv,
    swap_send, swap_recv, part_ss, part_rs, down_ss, down_rs, give_ss, give_rs, rise_ss, rise_rs, mix_ss, mix_rs,
):
    s = lax.axis_index("segment")
    c = lax.axis_index("ctx")
    y, z = c // 8, c % 8
    partner = (1 - y) * 8 + z
    above, below = (s + 1) % SEGS, (s + SEGS - 1) % SEGS

    def ring_peer(delta):
        return y * 8 + (z + delta + 8) % 8

    peers = (ring_peer(1), ring_peer(-1))

    loads = [
        pltpu.make_async_copy(x_in, xs.at[0], load.at[0]),
        pltpu.make_async_copy(qkv_in, stage_qkv, load.at[1]),
        pltpu.make_async_copy(out_in, wo.at[0, pl.ds(0, HEAD), :], load.at[2]),
        pltpu.make_async_copy(skip_in, wsk.at[pl.ds(pl.multiple_of(z * ROWS, 16), ROWS), :], load.at[3]),
        pltpu.make_async_copy(up_in, xs.at[2], load.at[4]),
        pltpu.make_async_copy(bank_in, bank, load.at[5]),
        pltpu.make_async_copy(queue_in, queue, load.at[6]),
    ]
    for copy in loads:
        copy.start()

    barrier = pltpu.get_barrier_semaphore()
    diagonal = {"segment": (s + SEGS + 1 - 2 * y) % SEGS, "ctx": partner}
    greet = [{"ctx": ring_peer(d)} for d in (1, -1)]
    greet += [{"ctx": partner}, {"segment": above}, {"segment": below}, diagonal]
    for peer in greet:
        pl.semaphore_signal(barrier, inc=1, device_id=peer, device_id_type=MESH)

    pad = HP - HEAD
    wo[:, HEAD:HP, :] = jnp.zeros((2 * RING, pad, D), BF)
    for block in range(5):
        wqv[block * HP + HEAD : (block + 1) * HP, :] = jnp.zeros((pad, D), BF)
    wk[HEAD:128, :] = jnp.zeros((128 - HEAD, D), BF)
    kt[:, HEAD:128, :] = jnp.zeros((2, 128 - HEAD, 1024), BF)
    qt[:, :, HEAD:128, :] = jnp.zeros((2, 2, 128 - HEAD, 1024), BF)
    mt[:, :, :, HEAD:HP, :] = jnp.zeros((2, 2, RING, pad, TOK), BF)
    ones = (lax.broadcasted_iota(jnp.int32, (pad, 2048), 0) == 0).astype(F32).astype(BF)
    for t in range(2):
        vt[t, HEAD:HP, :] = ones

    gain_down, gain_up = gains[0:1, :], gains[1:2, :]
    loads[0].wait()
    act[0, 0] = layer_norm(xs[0].astype(F32), gain_down).astype(BF)
    loads[1].wait()
    wqv[0:HEAD, :] = stage_qkv[0]
    wqv[HP : HP + HEAD, :] = stage_qkv[2]
    wk[0:HEAD, :] = stage_qkv[1]
    loads[4].wait()
    loads[5].wait()
    skip_first = bank[slots[0, 0]]
    skip_second = bank[slots[0, 1]]
    rising = xs[2]
    operand[0, 0:TOK, :] = jnp.where(y == 0, rising, skip_first)
    give[0] = jnp.where(y == 0, skip_first, rising)
    give[1] = skip_second

    @pl.when(y == 1)
    def _():
        operand[1, 0:TOK, :] = skip_second

    def act_ring(t):
        return slot_ring(
            peers, act_send.at[t], act_recv.at[t],
            lambda p, half: act.at[t, p, pl.ds(half * 64, 64), :],
        )

    rings = [act_ring(0), act_ring(1)]
    out_ring = slot_ring(peers, wo_send, wo_recv, lambda p, half: wo.at[p, pl.ds(half * 48, 40 if half else 48), :])
    skip_ring = row_ring(peers, wsk_send, wsk_recv, z, wsk)

    def to_partner(src, dst, send, recv):
        return pltpu.make_async_remote_copy(
            src, dst, send, recv, device_id={"ctx": partner}, device_id_type=MESH
        )

    w_copies = [
        to_partner(wqv.at[pl.ds(0, HEAD), :], wqv.at[pl.ds(2 * HP, HEAD), :], w_send.at[0], w_recv.at[0]),
        to_partner(wqv.at[pl.ds(HP, HEAD), :], wqv.at[pl.ds(3 * HP, HEAD), :], w_send.at[1], w_recv.at[1]),
        to_partner(wk.at[pl.ds(0, HEAD), :], wqv.at[pl.ds(4 * HP, HEAD), :], w_send.at[2], w_recv.at[2]),
    ]
    give_copies = [
        to_partner(give.at[t], operand.at[t, pl.ds(TOK, TOK), :], give_ss.at[t], give_rs.at[t])
        for t in range(2)
    ]

    pl.semaphore_wait(barrier, len(greet))
    rings[0].begin(0)
    rings[0].begin(1)
    for copy in w_copies:
        copy.start()

    def pair_copies(t, g):
        lo, hi = GROUPS[g]
        n = (hi - lo) * TOK
        return [
            to_partner(
                qs.at[t, :, pl.ds(lo * TOK, n)],
                qt.at[t, 1, pl.ds(0, HEAD), pl.ds(lo * TOK, n)],
                pair_send.at[t, g, 0], pair_recv.at[t, g, 0],
            ),
            to_partner(
                ks.at[t, :, pl.ds(lo * TOK, n)],
                kt.at[t, pl.ds(0, HEAD), pl.ds(lo * TOK, n)],
                pair_send.at[t, g, 1], pair_recv.at[t, g, 1],
            ),
            to_partner(
                vs.at[t, :, pl.ds(lo * TOK, n)],
                vt.at[t, pl.ds(0, HEAD), pl.ds(1024 + lo * TOK, n)],
                pair_send.at[t, g, 2], pair_recv.at[t, g, 2],
            ),
        ]

    def project(t, g):
        lo, hi = GROUPS[g]
        n = (hi - lo) * TOK
        tokens = act[t, lo:hi].reshape(n, D)
        made = nt(wqv[...], tokens)
        keys = nt(tokens, wk[...]).astype(BF)
        own_q = (made[0:HEAD] * (SCALE * LOG2E)).astype(BF)
        pair_q = (made[2 * HP : 2 * HP + HEAD] * (SCALE * LOG2E)).astype(BF)
        made = made.astype(BF)
        qt[t, 0, 0:HEAD, lo * TOK : hi * TOK] = own_q
        vt[t, 0:HEAD, lo * TOK : hi * TOK] = made[HP : HP + HEAD]
        qs[t, :, lo * TOK : hi * TOK] = pair_q
        vs[t, :, lo * TOK : hi * TOK] = made[3 * HP : 3 * HP + HEAD]
        ks[t, :, lo * TOK : hi * TOK] = made[4 * HP : 4 * HP + HEAD]
        kk[t, lo * TOK : hi * TOK, :] = keys
        for copy in pair_copies(t, g):
            copy.start()

    def turn_keys(t, lo, hi):
        for p in range(lo, hi):
            kk[t, 1024 + p * TOK : 1024 + (p + 1) * TOK, :] = kt[t, :, p * TOK : (p + 1) * TOK].T

    def head_copy(t, half, p, mirror, delta):
        ring = 1 - y if t == 1 and half == 1 else y
        return pltpu.make_async_remote_copy(
            ot.at[t, half, p], mt.at[t, half, mirror, pl.ds(0, HEAD), :],
            head_send.at[t, half, p], head_recv.at[t, half, mirror],
            device_id={"ctx": ring * 8 + (z + delta + 8) % 8}, device_id_type=MESH,
        )

    def swap_copy(p):
        return to_partner(
            wo.at[p, pl.ds(0, HEAD), :], wo.at[RING + p, pl.ds(0, HEAD), :], swap_send.at[p], swap_recv.at[p]
        )

    def attend_block(t, half, b):
        queries = qt[t, half, :, pl.ds(pl.multiple_of(b * 256, 256), 256)]
        peak = None
        for kb in range(8):
            made = jnp.dot(kk[t, kb * 256 : (kb + 1) * 256, :], queries, preferred_element_type=F32)
            scores[kb] = made
            top = jnp.max(made.reshape(32, 8, 256), axis=0)
            peak = top if peak is None else jnp.maximum(peak, top)
        peak = jnp.max(peak, axis=0, keepdims=True)
        total = jnp.zeros((HP, 256), F32)
        for kb in range(8):
            powers = jnp.exp2(scores[kb] - peak).astype(BF)
            total += jnp.dot(vt[t, :, kb * 256 : (kb + 1) * 256], powers, preferred_element_type=F32)
        return (total[0:HEAD] * (1.0 / total[HEAD : HEAD + 1, :])).astype(BF)

    def attend_early(b):
        queries = qt[1, 1, :, pl.ds(pl.multiple_of(b * 256, 256), 256)]
        peak = None
        for kb, (start, size) in enumerate(EARLY):
            made = jnp.dot(kk[1, start : start + size, :], queries, preferred_element_type=F32)
            scores[kb, 0:size, :] = made
            top = jnp.max(made.reshape(size // 8, 8, 256), axis=0)
            peak = top if peak is None else jnp.maximum(peak, top)
        peak = jnp.max(peak, axis=0, keepdims=True)
        total = jnp.zeros((HP, 256), F32)
        for kb, (start, size) in enumerate(EARLY):
            powers = jnp.exp2(scores[kb, 0:size, :] - peak).astype(BF)
            total += jnp.dot(vt[1, :, start : start + size], powers, preferred_element_type=F32)
        early_peak[b] = jnp.broadcast_to(peak, (8, 256))
        early_total[b] = total

    def attend_late(b):
        queries = qt[1, 1, :, pl.ds(pl.multiple_of(b * 256, 256), 256)]
        keys = jnp.concatenate([kk[1, 896:1024, :], kk[1, 1920:2048, :]], axis=0)
        values = jnp.concatenate([vt[1, :, 896:1024], vt[1, :, 1920:2048]], axis=1)
        made = jnp.dot(keys, queries, preferred_element_type=F32)
        before = early_peak[b][0:1, :]
        peak = jnp.maximum(before, jnp.max(jnp.max(made.reshape(32, 8, 256), axis=0), axis=0, keepdims=True))
        powers = jnp.exp2(made - peak).astype(BF)
        total = early_total[b] * jnp.exp2(before - peak)
        total += jnp.dot(values, powers, preferred_element_type=F32)
        return (total[0:HEAD] * (1.0 / total[HEAD : HEAD + 1, :])).astype(BF)

    def pass_on(t, half, b, made):
        ot[t, half, 2 * b + 1] = made[:, TOK : 2 * TOK]
        ot[t, half, 2 * b] = made[:, 0:TOK]
        head_copy(t, half, 2 * b + 1, 2 * b + 2 - b // 3, b + 1).start()

        @pl.when(b > 0)
        def _():
            head_copy(t, half, 2 * b, 2 * b - 1, -b).start()

    def attend(t, half, first, stop, between, block=None):
        def body(i, carry):
            b = 3 - i
            pass_on(t, half, b, attend_block(t, half, b) if block is None else block(b))
            for at, work in between.items():

                @pl.when(i == at)
                def _():
                    work()

            return carry

        lax.fori_loop(first, stop, body, 0)
        if stop == 4 and t == 1 and half == 1:
            head_copy(t, half, 0, 0, 0).start()
        elif stop == 4:
            mt[t, half, 0, 0:HEAD, :] = ot[t, half, 0]

    def part_copy(h):
        return to_partner(
            part_send.at[pl.ds(h * 64, 64), :], part_recv.at[pl.ds(h * 64, 64), :],
            part_ss.at[h], part_rs.at[h],
        )

    def heads_times_out(t, half, slots):
        for p in range(1 if t == 0 or half == 0 else 0, 8):
            head_copy(t, half, p, p, 1).wait_recv()
        weights = wo[slots : slots + RING].reshape(RING * HP, D)
        return tn(mt[t, half].reshape(RING * HP, TOK), weights)

    def project_pair():
        part_send[...] = heads_times_out(0, 1, 0).astype(BF)
        for h in range(2):
            part_copy(h).start()

    def finish(h, own):
        rows = slice(h * 64, (h + 1) * 64)
        part_copy(h).wait_recv()
        x1[0, rows, :] = (own[rows] + part_recv[rows, :].astype(F32)).astype(BF)

    def down_copy(h):
        return pltpu.make_async_remote_copy(
            x1.at[0, pl.ds(h * 64, 64), :], down.at[pl.ds(h * 64, 64), :],
            down_ss.at[h], down_rs.at[h], device_id={"segment": above}, device_id_type=MESH,
        )

    def rise_copy():
        return pltpu.make_async_remote_copy(
            asc_out.at[0], operand.at[1, pl.ds(pl.multiple_of(y * TOK, 16), TOK), :],
            rise_ss.at[0], rise_rs.at[y], device_id={"segment": below, "ctx": z}, device_id_type=MESH,
        )

    def turn_copy():
        return pltpu.make_async_remote_copy(
            x1.at[0], operand.at[1, pl.ds(TOK, TOK), :],
            rise_ss.at[1], rise_rs.at[1], device_id={"ctx": partner}, device_id_type=MESH,
        )

    def mix_copy(t):
        return to_partner(asc_send.at[t], asc_recv.at[t], mix_ss.at[t], mix_rs.at[t])

    def ascend_first(t):
        asc_send[t] = jnp.dot(operand[t, TOK : 2 * TOK, :], wsk[...], preferred_element_type=F32).astype(BF)
        own_up[...] = jnp.dot(operand[t, 0:TOK, :], wsk[...], preferred_element_type=F32)

    def ascend_last(t):
        mix_copy(t).wait_recv()
        asc_out[t] = layer_norm(own_up[...] + asc_recv[t].astype(F32), gain_up).astype(BF)
        pltpu.make_async_copy(asc_out.at[t], asc_ref.at[t], store.at[1, t]).start()

    for j in range(4):
        rings[0].step(j)
    for copy in w_copies:
        copy.wait_recv()
    for g in range(3):
        project(0, g)
    rings[0].step(4)
    rings[0].step(5)
    loads[2].wait()
    out_ring.begin(0)
    project(0, 3)
    rings[0].step(6)
    out_ring.begin(1)
    project(0, 4)
    for g in range(5):
        for copy in pair_copies(0, g):
            copy.wait_recv()
    turn_keys(0, 0, 8)
    swap_copy(0).start()

    def out_step(j):
        def work():
            out_ring.step(j)
            if j % 2:
                swap_copy(j).start()
                swap_copy(j + 1).start()

        return work

    attend(0, 1, 0, 4, {1: out_step(0), 3: out_step(1)})
    attend(0, 0, 0, 4, {1: out_step(2), 3: out_step(3)})
    loads[3].wait()
    out_ring.step(4)
    out_ring.step(5)
    skip_ring.begin(0)
    out_ring.step(6)
    skip_ring.begin(1)
    project_pair()
    own = heads_times_out(0, 0, 0) + xs[0].astype(F32)
    skip_ring.step(0)
    skip_ring.step(1)
    for h in range(2):
        finish(h, own)
        down_copy(h).start()
    for p in range(5, 8):
        swap_copy(p).start()
    give_copies[0].start()
    pl.when(y == 0)(lambda: give_copies[1].start())
    pltpu.make_async_copy(x1.at[0], desc_ref.at[0], store.at[0, 0]).start()

    last = s == SEGS - 1

    @pl.when(jnp.logical_and(last, y == 0))
    def _():
        operand[1, 0:TOK, :] = x1[0]

    @pl.when(jnp.logical_and(last, y == 1))
    def _():
        turn_copy().start()

    skip_ring.step(2)
    skip_ring.step(3)
    loads[6].wait()
    entering = queue[entry[0]]
    for h in range(2):
        rows = slice(h * 64, (h + 1) * 64)
        down_copy(h).wait_recv()
        xs[1, rows, :] = jnp.where(s == 0, entering[rows], down[rows, :])
        act[1, 0, rows, :] = layer_norm(xs[1, rows, :].astype(F32), gain_down).astype(BF)
    project(1, 0)
    skip_ring.step(4)
    rings[1].begin(0)
    skip_ring.step(5)
    rings[1].begin(1)
    skip_ring.step(6)

    give_copies[0].wait_recv()
    ascend_first(0)
    mix_copy(0).start()
    rings[1].step(0)
    rings[1].step(1)
    project(1, 1)
    rings[1].step(2)
    rings[1].step(3)
    project(1, 2)
    ascend_last(0)
    pl.when(s > 0)(lambda: rise_copy().start())

    @pl.when(y == 1)
    def _():
        give_copies[1].wait_recv()
        ascend_first(1)

    rings[1].step(4)
    rings[1].step(5)
    project(1, 3)
    rings[1].step(6)
    project(1, 4)

    @pl.when(jnp.logical_and(y == 0, s < SEGS - 1))
    def _():
        pltpu.make_async_remote_copy(
            asc_out.at[0], operand.at[1, pl.ds(0, TOK), :], rise_ss.at[0], rise_rs.at[0],
            device_id={"segment": below, "ctx": z}, device_id_type=MESH,
        ).wait_recv()

    @pl.when(y == 0)
    def _():
        turn_copy().wait_recv()
        ascend_first(1)

    for g in range(4):
        for copy in pair_copies(1, g):
            copy.wait_recv()
    turn_keys(1, 0, 7)

    def early(i, carry):
        attend_early(2 - i)
        return carry

    mix_copy(1).start()
    lax.fori_loop(0, 3, early, 0)
    for copy in pair_copies(1, 4):
        copy.wait_recv()
    turn_keys(1, 7, 8)
    attend(1, 1, 0, 1, {})
    attend(1, 1, 1, 4, {}, attend_late)
    attend(1, 0, 0, 4, {})
    for p in range(8):
        swap_copy(p).wait_recv()
    own = heads_times_out(1, 1, RING) + xs[1].astype(F32)
    x1[1] = (own + heads_times_out(1, 0, 0)).astype(BF)
    pltpu.make_async_copy(x1.at[1], desc_ref.at[1], store.at[0, 1]).start()
    ascend_last(1)

    for ring in (*rings, out_ring, skip_ring):
        ring.drain()
    for copy in w_copies:
        copy.wait_send()
    give_copies[0].wait_send()
    pl.when(y == 0)(lambda: give_copies[1].wait_send())
    for t in range(2):
        for g in range(5):
            for copy in pair_copies(t, g):
                copy.wait_send()
        mix_copy(t).wait_send()
        for half in range(2):
            for p in range(1 if t == 0 or half == 0 else 0, 8):
                head_copy(t, half, p, p, 1).wait_send()
    for p in range(8):
        swap_copy(p).wait_send()
    for h in range(2):
        part_copy(h).wait_send()
        down_copy(h).wait_send()
    pl.when(s > 0)(lambda: rise_copy().wait_send())
    pl.when(jnp.logical_and(last, y == 1))(lambda: turn_copy().wait_send())
    for t in range(2):
        pltpu.make_async_copy(x1.at[t], desc_ref.at[t], store.at[0, t]).wait()
        pltpu.make_async_copy(asc_out.at[t], asc_ref.at[t], store.at[1, t]).wait()


def hand_on(desc_in, asc_in, desc_ref, asc_ref, held, read, write):
    ends = ((desc_in, desc_ref), (asc_in, asc_ref))
    pieces = [(a, t, h) for t in range(2) for a in range(2) for h in range(2)]

    def fetch(a, t, h):
        rows = pl.ds(h * 64, 64)
        return pltpu.make_async_copy(ends[a][0].at[t, rows, :], held.at[a, t, rows, :], read.at[a, t, h])

    def put(a, t, h):
        rows = pl.ds(h * 64, 64)
        return pltpu.make_async_copy(held.at[a, t, rows, :], ends[a][1].at[t, rows, :], write.at[a, t, h])

    for piece in pieces:
        fetch(*piece).start()
    for piece in pieces:
        fetch(*piece).wait()
        put(*piece).start()
    for piece in pieces:
        put(*piece).wait()


def on_device(
    carried_down, carried_up, skip_bank, queue, next_entry, skip_slot, w_qkv, w_out, w_skip, gains
):
    hbm = pl.BlockSpec(memory_space=pl.ANY)
    smem = pl.BlockSpec(memory_space=pltpu.SMEM)
    vmem = pl.BlockSpec(memory_space=pltpu.VMEM)
    dma = pltpu.SemaphoreType.DMA
    V = pltpu.VMEM
    scratch = [
        V((3, TOK, D), BF),
        V((TOK, D), BF),
        V((3, TOK, D), BF),
        V((8, TOK, D), BF),
        V((3, HEAD, D), BF),
        V((2, RING, TOK, D), BF),
        V((5 * HP, D), BF),
        V((TOK, D), BF),
        V((2, 2, 128, 1024), BF),
        V((2, 2048, 128), BF),
        V((2, HP, 2048), BF),
        V((2, HEAD, 1024), BF),
        V((2, HEAD, 1024), BF),
        V((2, 128, 1024), BF),
        V((2, HEAD, 1024), BF),
        V((8, 256, 256), F32),
        V((2, 2, RING, HEAD, TOK), BF),
        V((2, 2, RING, HP, TOK), BF),
        V((2 * RING, HP, D), BF),
        V((D, D), BF),
        V((TOK, D), BF),
        V((TOK, D), BF),
        V((2, TOK, D), BF),
        V((2, 2 * TOK, D), BF),
        V((2, TOK, D), BF),
        V((2, TOK, D), BF),
        V((2, TOK, D), BF),
        V((2, TOK, D), BF),
        V((TOK, D), F32),
        V((3, 8, 256), F32),
        V((3, HP, 256), F32),
        dma((7,)), dma((2, 2)),
        dma((2, 2, 7)), dma((2, 2, 7)), dma((2, 7)), dma((2, 7)), dma((2, 7)), dma((2, 7)),
        dma((2, 5, 3)), dma((2, 5, 3)), dma((3,)), dma((3,)), dma((2, 2, 8)), dma((2, 2, 8)),
        dma((8,)), dma((8,)), dma((2,)), dma((2,)), dma((2,)), dma((2,)), dma((2,)), dma((2,)),
        dma((2,)), dma((2,)), dma((2,)), dma((2,)),
    ]
    desc, asc = pl.pallas_call(
        kernel,
        out_shape=(
            jax.ShapeDtypeStruct((2, TOK, D), BF),
            jax.ShapeDtypeStruct((2, TOK, D), BF),
        ),
        in_specs=[hbm, hbm, hbm, hbm, smem, smem, hbm, hbm, hbm, vmem],
        out_specs=(hbm, hbm),
        scratch_shapes=scratch,
        compiler_params=pltpu.CompilerParams(
            collective_id=0, has_side_effects=True, vmem_limit_bytes=60 * 1024 * 1024
        ),
    )(
        carried_down[0], carried_up[0], skip_bank[0], queue, next_entry, skip_slot.T,
        w_qkv[0], w_out[0], w_skip[0], gains[0],
    )
    desc, asc = pl.pallas_call(
        hand_on,
        out_shape=(
            jax.ShapeDtypeStruct((2, TOK, D), BF),
            jax.ShapeDtypeStruct((2, TOK, D), BF),
        ),
        in_specs=[hbm, hbm],
        out_specs=(hbm, hbm),
        scratch_shapes=[V((2, 2, TOK, D), BF), dma((2, 2, 2)), dma((2, 2, 2))],
        compiler_params=pltpu.CompilerParams(vmem_limit_bytes=60 * 1024 * 1024),
    )(desc, asc)
    return desc[:, None], asc[:, None]


def solution(mesh):
    in_specs = (
        P("segment", "ctx", None),
        P("segment", "ctx", None),
        P("segment", None, "ctx", None),
        P(None, "ctx", None),
        P(),
        P(None, "segment"),
        P("segment", None, "ctx", None),
        P("segment", "ctx", None),
        P("segment", "ctx", None),
        P("segment", None, None),
    )
    out_specs = (P(None, "segment", "ctx", None), P(None, "segment", "ctx", None))
    return jax.shard_map(
        on_device, mesh=mesh, in_specs=in_specs, out_specs=out_specs, check_vma=False
    )
```
